32 devices in a mesh: col: 4 (over y, core), fac: 8 (over z, x).
Axes of the slice: x: 2, y: 2, z: 4, core: 2. Of those that a mesh axis runs over, the one named last changes fastest.
Arguments:
- facets: bfloat16 [2, 4096, 4096], P(None, 'col', 'fac'), may hold values from -6 to 6
- row_taper: float32 [4096], P('col'), may hold values from 0.5 to 1.5
- column_taper: float32 [4096], replicated, may hold values from 0.5 to 1.5
- column_place: int32 [1], replicated, may hold values from 0 to 511
- row_offset: int32 [4], replicated, may hold values from 0 to 4095
- column_offset: int32 [8], replicated, may hold values from 0 to 4095
- slot_subgrid: int32 [4, 8], replicated, may hold values from 0 to 7, each once within a row
Outputs:
- subgrids: float32 [4, 8, 2, 512, 128], P('col', 'fac')
The draws below stay inside these ranges and needn't reach their ends.
All inputs are finite; a program needn't handle non-finite values.
Results may differ from the reference program's by a relative error of at most 0.0052.
Values may be sent and summed in bfloat16 or wider, within the bound.
A program may use at most 64 MiB of HBM per device.

```python
import math
import jax
import jax.numpy as jnp
from jax import lax

FACET = 4096
STRIP = 128
SUBGRID = 512
FACET_COLS = 1
IMG_COLS = 4096
N_COL = 4
N_FAC = 8


def touch_ends(drawn, key, low, high):
    longest = drawn.shape.index(max(drawn.shape))
    spots = []
    for shift in (0, 1):
        where = [jax.random.randint(jax.random.fold_in(key, axis), (), 0, length) for axis, length in enumerate(drawn.shape)]
        where[longest] = (where[longest] + shift) % drawn.shape[longest]
        spots.append(tuple(where))
    return drawn.at[spots[0]].set(low).at[spots[1]].set(high)


def level_of(own_key, dims, cuts, least, high):
    factor_of, own = 1.0, jax.random.fold_in(own_key, 6)
    for position, blocks in cuts:
        heights = jnp.exp(jax.random.uniform(jax.random.fold_in(own, position), (blocks,), jnp.float32, least / len(cuts), high / len(cuts)))
        factor_of = factor_of * jnp.repeat(heights, dims[position] // blocks).reshape([-1 if axis == position else 1 for axis in range(len(dims))])
    return factor_of


def centred(key, extent, scale, bound, split=(), held_as=jnp.bfloat16):
    gain = level_of(key, extent, split, -0.22, 0.18) if split else 1.0
    result = jax.random.normal(key, extent, jnp.float32) * scale * gain
    return jnp.minimum(jnp.maximum(result, -bound), bound).astype(held_as)


def setup_inputs(seed: int = 0) -> dict:
    keys = jax.random.split(jax.random.key(seed), 8)
    facets = centred(keys[0], (2, FACET, IMG_COLS), 1.0, 6.0, ((1, 4), (2, 8)))
    row_taper = jnp.clip(0.5 + 1.0 * jax.random.uniform(keys[1], (FACET,), jnp.float32) ** level_of(keys[1], (FACET,), ((0, 4),), -0.2, 0.2), 0.5, 1.5)
    column_taper = jnp.clip(jax.random.uniform(keys[2], (FACET,), jnp.float32, 0.5, 1.5), 0.5, 1.5)
    column_place = jax.random.randint(keys[3], (FACET_COLS,), 0, SUBGRID).astype(jnp.int32)
    row_offset = touch_ends(jax.random.randint(keys[4], (N_COL,), 0, FACET), jax.random.fold_in(keys[4], 1), 0, FACET - 1).astype(jnp.int32)
    column_offset = touch_ends(jax.random.randint(keys[5], (N_FAC,), 0, FACET), jax.random.fold_in(keys[5], 1), 0, FACET - 1).astype(jnp.int32)
    slot_subgrid = jax.vmap(lambda own: jax.random.permutation(own, N_FAC))(jax.random.split(keys[6], N_COL)).reshape((N_COL, N_FAC)).astype(jnp.int32)
    return {"facets": facets, "row_taper": row_taper, "column_taper": column_taper, "column_place": column_place, "row_offset": row_offset, "column_offset": column_offset, "slot_subgrid": slot_subgrid}


def phase_table(starts, positions):
    offsets = jnp.arange(STRIP, dtype=jnp.int32)
    frequency = (starts[:, None] + offsets[None, :]) % FACET
    phases = frequency[:, :, None] * positions[None, None, :] % FACET
    angles = phases.astype(jnp.float32) * (2.0 * math.pi / FACET)
    norm_scale = 1.0 / math.sqrt(FACET)
    return jnp.stack([jnp.cos(angles) * norm_scale, -jnp.sin(angles) * norm_scale]).astype(jnp.bfloat16)

def complex_rows(table_rows, real_part, imag_part):
    row_total = table_rows.shape[1]
    stacked = table_rows.reshape(2 * row_total, table_rows.shape[2])
    first_product = jnp.dot(stacked, real_part, preferred_element_type=jnp.float32)
    second = jnp.dot(stacked, imag_part, preferred_element_type=jnp.float32)
    return (first_product[:row_total] - second[row_total:], second[:row_total] + first_product[row_total:])

def complex_cols(table_rows, real_part, imag_part):
    row_total = table_rows.shape[1]
    stacked = table_rows.reshape(2 * row_total, table_rows.shape[2])
    contract_dims = (((1,), (1,)), ((), ()))
    first_product = lax.dot_general(stacked, real_part, contract_dims, preferred_element_type=jnp.float32)
    second = lax.dot_general(stacked, imag_part, contract_dims, preferred_element_type=jnp.float32)
    return (first_product[:row_total] - second[row_total:], second[:row_total] + first_product[row_total:])

def reference(facets, row_taper, column_taper, column_place, row_offset, column_offset, slot_subgrid):
    column_gain = jnp.tile(column_taper, FACET_COLS)
    prepared = (facets.astype(jnp.float32) * row_taper[None, :, None] * column_gain[None, None, :]).astype(jnp.bfloat16)
    positions = jnp.arange(FACET, dtype=jnp.int32)
    offsets = jnp.arange(STRIP, dtype=jnp.int32)
    column_targets = (column_place[:, None] + offsets[None, :]) % SUBGRID

    def one_group(column_group):
        encode = phase_table(row_offset[column_group][None], positions)[:, 0]
        real_out, imag_out = complex_rows(encode, prepared[0], prepared[1])
        strip = lax.optimization_barrier(jnp.stack([real_out, imag_out]).astype(jnp.bfloat16))
        starts = column_offset[slot_subgrid[column_group]]
        decode = phase_table(starts, positions).reshape(2, N_FAC * STRIP, FACET)

        def add_facet(summed, facet_col):
            part_real = lax.dynamic_slice_in_dim(strip[0], facet_col * FACET, FACET, 1)
            part_imag = lax.dynamic_slice_in_dim(strip[1], facet_col * FACET, FACET, 1)
            real_part, imag_part = complex_cols(decode, part_real, part_imag)
            contribution = jnp.stack([real_part.reshape(N_FAC, STRIP, STRIP), imag_part.reshape(N_FAC, STRIP, STRIP)], axis=1)
            summed = summed.at[:, :, column_targets[facet_col], :].add(contribution)
            return (summed, None)
        summed, unused = lax.scan(add_facet, jnp.zeros((N_FAC, 2, SUBGRID, STRIP), jnp.float32), jnp.arange(FACET_COLS, dtype=jnp.int32))
        return summed
    return lax.map(one_group, jnp.arange(N_COL, dtype=jnp.int32))
```

```python
import functools
import math

import jax
import jax.numpy as jnp
from jax import lax
from jax.experimental import pallas as pl
from jax.experimental.pallas import tpu as pltpu
from jax.sharding import PartitionSpec as P

FACET = 4096
STRIP = 128
SUBGRID = 512
FINE = 16
SIZES = (32, 32, 32, 32)
CHUNKS = len(SIZES)
PIECES = 2
HOP_ROWS = 60
MESH = pl.DeviceIdType.MESH


def unit_phase(phases):
    quarter = FACET // 4
    shifted = phases + quarter // 2
    angle = ((shifted & (quarter - 1)) - quarter // 2).astype(jnp.float32) * (2.0 * math.pi / FACET)
    turn = lax.shift_right_logical(shifted & (FACET - 1), quarter.bit_length() - 1)
    sq = angle * angle
    cosine = 1.0 + sq * (-1 / 2 + sq * (1 / 24 + sq * (-1 / 720 + sq * (1 / 40320))))
    sine = angle * (1.0 + sq * (-1 / 6 + sq * (1 / 120 + sq * (-1 / 5040 + sq * (1 / 362880)))))
    odd = (turn & 1) == 1
    first = jnp.where(odd, sine, cosine)
    second = jnp.where(odd, cosine, sine)
    real = jnp.where(((turn + 1) & 2) == 2, -first, first)
    imag = jnp.where((turn & 2) == 2, second, -second)
    return real, imag


def span(j):
    start = 2 * sum(SIZES[:j])
    return slice(start, start + 2 * SIZES[j])


def order():
    far_done, free, events = 0, 0, []
    for j, size in enumerate(SIZES):
        far_done += size
        free = max(free, far_done) + size
        events += [(far_done, 0, j), (free + HOP_ROWS, 1, j)]
    return [event[1:] for event in sorted(events)]


def iota(shape, dim):
    return lax.broadcasted_iota(jnp.int32, shape, dim)


def kernel(
    cols, facs,
    row_offset_in, column_offset_in, slot_subgrid_in, row_taper_in, column_taper_in, facets,
    out,
    row_offset, column_offset, slot_subgrid, row_taper, column_gain, held, coarse_r, coarse_i, fine_r, fine_i, steep_r, steep_i, encode, decode_r, decode_i,
    pair_out, pair_in, far_part, far_out, far_in, own_part, strip, strip_in,
    half, mine, slots_out, slots_in,
    small_sem, held_sem, pair_send, pair_recv, far_send, far_recv, strip_send, strip_recv, slot_send, slot_recv,
):
    col = lax.axis_index("col")
    fac = lax.axis_index("fac")
    col_hi, core = col // 2, col % 2
    fac_hi, fac_lo = fac // 2, fac % 2
    highs, zs = cols // 2, facs // 2
    rows, width = facets.shape[1], facets.shape[2]

    pair_id = (col_hi * 2 + 1 - core, fac)
    far_ids = [((col_hi + d) % highs * 2 + core, fac) for d in range(1, highs)]
    strip_id = (col, fac_hi * 2 + 1 - fac_lo)
    slot_ids = [(col, (fac_hi + d) % zs * 2 + fac_lo) for d in range(1, zs)]
    peers = [pair_id, *far_ids, strip_id, *slot_ids]
    own_columns = pl.ds(pl.multiple_of(fac * width, width), width)
    small = [
        pltpu.make_async_copy(source, target, small_sem.at[n])
        for n, (source, target) in enumerate((
            (row_offset_in, row_offset), (column_offset_in, column_offset), (slot_subgrid_in, slot_subgrid),
            (row_taper_in, row_taper),
            (column_taper_in.at[:, own_columns], column_gain)))]
    depth = rows // PIECES
    pieces = [slice(n * depth, (n + 1) * depth) for n in range(PIECES)]
    loads = [pltpu.make_async_copy(facets.at[:, piece], held.at[:, piece], held_sem.at[n]) for n, piece in enumerate(pieces)]
    for load in (*small, *loads):
        load.start()
    barrier = pltpu.get_barrier_semaphore()
    for peer in peers:
        pl.semaphore_signal(barrier, inc=1, device_id=peer, device_id_type=MESH)

    steps = STRIP // FINE
    position = col * rows + iota((1, rows), 1)
    fine_r[...], fine_i[...] = unit_phase(iota((FINE, rows), 0) * position)
    for load in small:
        load.wait()
    gain = row_taper[...] * (1.0 / math.sqrt(FACET))

    def encode_group(index, group):
        first = (row_offset[group] + FINE * iota((steps, rows), 0)) & (FACET - 1)
        real, imag = unit_phase(first * position)
        coarse_r[...] = real * gain
        coarse_i[...] = imag * gain

        def row(i, carry):
            ar, ai = coarse_r[pl.ds(i, 1), :], coarse_i[pl.ds(i, 1), :]
            br, bi = fine_r[...], fine_i[...]
            at = pl.multiple_of(i * FINE, FINE)
            encode[index, pl.ds(at, FINE), :] = (ar * br - ai * bi).astype(jnp.bfloat16)
            encode[index, pl.ds(at + STRIP, FINE), :] = (ar * bi + ai * br).astype(jnp.bfloat16)
            return carry

        lax.fori_loop(0, steps, row, 0)

    def combined(by_real, by_imag):
        return by_real[:STRIP] - by_imag[STRIP:], by_imag[:STRIP] + by_real[STRIP:]

    def product(index):
        table = encode[index]
        return combined(*[jnp.dot(table, held[p], preferred_element_type=jnp.float32) for p in range(2)])

    def first_product(index):
        sums = [None, None]
        for load, piece in zip(loads, pieces):
            load.wait()
            table = encode[index, :, piece]
            for p in range(2):
                term = jnp.dot(table, held[p, piece], preferred_element_type=jnp.float32)
                sums[p] = term if sums[p] is None else sums[p] + term
        return combined(*sums)

    def chunked(target, real, imag):
        for j, size in enumerate(SIZES):
            start = span(j).start
            target[start:start + size] = real[start // 2:start // 2 + size].astype(target.dtype)
            target[start + size:start + 2 * size] = imag[start // 2:start // 2 + size].astype(target.dtype)

    def pair_copy(d, j):
        return pltpu.make_async_remote_copy(
            src_ref=pair_out.at[d, span(j)], dst_ref=pair_in.at[d, span(j)], send_sem=pair_send.at[d, j],
            recv_sem=pair_recv.at[d, j], device_id=pair_id, device_id_type=MESH)

    def far_copy(d, j):
        return pltpu.make_async_remote_copy(
            src_ref=far_out.at[d - 1, span(j)], dst_ref=far_in.at[d - 1, span(j)], send_sem=far_send.at[d - 1, j],
            recv_sem=far_recv.at[d - 1, j], device_id=far_ids[d - 1], device_id_type=MESH)

    def strip_copy(j):
        return pltpu.make_async_remote_copy(
            src_ref=strip.at[span(j)], dst_ref=strip_in.at[span(j)], send_sem=strip_send.at[j],
            recv_sem=strip_recv.at[j], device_id=strip_id, device_id_type=MESH)

    def slot_copy(d, j):
        return pltpu.make_async_remote_copy(
            src_ref=slots_out.at[d - 1, span(j)], dst_ref=slots_in.at[d - 1, span(j)], send_sem=slot_send.at[d - 1, j],
            recv_sem=slot_recv.at[d - 1, j], device_id=slot_ids[d - 1], device_id_type=MESH)

    def group(d, own):
        encode_group(2 * d + own, (col_hi + d) % highs * 2 + (core if own else 1 - core))

    for d in range(1, highs):
        group(d, 0)
        group(d, 1)
    for d in range(1, highs):
        chunked(pair_out.at[d], *(first_product(2 * d) if d == 1 else product(2 * d)))
        if d == 1:
            pl.semaphore_wait(barrier, len(peers))
        for j in range(CHUNKS):
            pair_copy(d, j).start()
        chunked(far_part.at[d - 1], *product(2 * d + 1))
    for d in range(1, highs):
        for j in range(CHUNKS):
            pair_copy(d, j).wait_recv()
            far_out[d - 1, span(j)] = (
                far_part[d - 1, span(j)] + pair_in[d, span(j)].astype(jnp.float32)).astype(jnp.bfloat16)
            far_copy(d, j).start()
    group(0, 0)
    chunked(pair_out.at[0], *product(0))
    for j in range(CHUNKS):
        pair_copy(0, j).start()
    group(0, 1)
    chunked(own_part, *product(1))

    lanes = zs * STRIP
    coarse_n = width // FINE
    starts = []
    for d in range(zs):
        start = column_offset[slot_subgrid[col, (fac_hi + d) % zs * 2 + fac_lo]]
        starts.append((start + iota((1, STRIP), 1)) & (FACET - 1))
    frequency = jnp.concatenate(starts, axis=1)
    fine_real, fine_imag = unit_phase(iota((FINE, lanes), 0) * frequency)
    fine_real, fine_imag = fine_real * (1.0 / math.sqrt(FACET)), fine_imag * (1.0 / math.sqrt(FACET))
    for part, block in enumerate((fac, fac_hi * 2 + 1 - fac_lo)):
        base = part * width
        steep_r[...], steep_i[...] = unit_phase((block * width + FINE * iota((coarse_n, lanes), 0)) * frequency)

        def row(i, carry, base=base):
            ar, ai = steep_r[pl.ds(i, 1), :], steep_i[pl.ds(i, 1), :]
            at = pl.multiple_of(base + i * FINE, FINE)
            decode_r[pl.ds(at, FINE), :] = (ar * fine_real - ai * fine_imag).astype(jnp.bfloat16)
            decode_i[pl.ds(at, FINE), :] = (ar * fine_imag + ai * fine_real).astype(jnp.bfloat16)
            return carry

        lax.fori_loop(0, coarse_n, row, 0)

    def decoded(block, part):
        at = slice(part * width, (part + 1) * width)
        size = block.shape[0] // 2
        by_real = jnp.dot(block, decode_r[at], preferred_element_type=jnp.float32)
        by_imag = jnp.dot(block, decode_i[at], preferred_element_type=jnp.float32)
        return jnp.concatenate([by_real[:size] - by_imag[size:], by_imag[:size] + by_real[size:]], axis=0)

    def begin(j):
        pair_copy(0, j).wait_recv()
        total = own_part[span(j)] + pair_in[0, span(j)].astype(jnp.float32)
        for d in range(1, highs):
            far_copy(d, j).wait_recv()
            total = total + far_in[d - 1, span(j)].astype(jnp.float32)
        strip[span(j)] = (total * column_gain[...]).astype(jnp.bfloat16)
        strip_copy(j).start()
        half[span(j)] = decoded(strip[span(j)], 0)

    def finish(j):
        strip_copy(j).wait_recv()
        total = half[span(j)] + decoded(strip_in[span(j)], 1)
        mine[span(j)] = total[:, :STRIP]
        for d in range(1, zs):
            slots_out[d - 1, span(j)] = total[:, d * STRIP:(d + 1) * STRIP].astype(jnp.bfloat16)
            slot_copy(d, j).start()

    for stage, j in order():
        (begin, finish)[stage](j)

    sums = []
    for j in range(CHUNKS):
        total = mine[span(j)]
        for d in range(1, zs):
            slot_copy(d, j).wait_recv()
            total = total + slots_in[d - 1, span(j)].astype(jnp.float32)
        sums.append(total)
    for part in range(2):
        value = jnp.concatenate([s[part * size:(part + 1) * size] for s, size in zip(sums, SIZES)], axis=0)
        out[part] = value.T

    for j in range(CHUNKS):
        for d in range(highs):
            pair_copy(d, j).wait_send()
        for d in range(1, highs):
            far_copy(d, j).wait_send()
        strip_copy(j).wait_send()
        for d in range(1, zs):
            slot_copy(d, j).wait_send()


def place_kernel(place, part, out, grid, sem):
    shift = lax.rem(place[0], 8)
    first = pl.multiple_of(place[0] - shift, 8)
    band = STRIP + 8
    copies = [pltpu.make_async_copy(grid.at[n, pl.ds(0, SUBGRID)], out.at[n], sem.at[n]) for n in range(2)]
    for n in range(2):
        grid[n] = jnp.zeros(grid.shape[1:], jnp.float32)
        grid[n, pl.ds(first, band)] = pltpu.roll(
            jnp.concatenate([part[n], jnp.zeros((8, STRIP), jnp.float32)], axis=0), shift, 0)
        grid[n, :band] += grid[n, SUBGRID:]
        copies[n].start()
    for copy in copies:
        copy.wait()


def solution(mesh):
    cols, facs = mesh.shape["col"], mesh.shape["fac"]
    highs, zs = cols // 2, facs // 2

    def on_device(facets, row_taper, column_taper, column_place, row_offset, column_offset, slot_subgrid):
        rows, width = facets.shape[1], facets.shape[2]
        bf16, f32 = jnp.bfloat16, jnp.float32
        lanes = zs * STRIP
        part = (2 * STRIP, width)
        slot = (2 * STRIP, STRIP)
        far = max(highs - 1, 1)
        sem = pltpu.SemaphoreType.DMA
        grid = pl.pallas_call(
            functools.partial(kernel, cols, facs),
            out_shape=jax.ShapeDtypeStruct((2, STRIP, STRIP), f32),
            in_specs=[pl.BlockSpec(memory_space=pltpu.HBM)] * 6,
            out_specs=pl.BlockSpec(memory_space=pltpu.VMEM),
            scratch_shapes=[
                pltpu.SMEM(row_offset.shape, jnp.int32), pltpu.SMEM(column_offset.shape, jnp.int32),
                pltpu.SMEM(slot_subgrid.shape, jnp.int32),
                pltpu.VMEM((1, rows), f32), pltpu.VMEM((1, width), f32),
                pltpu.VMEM((2, rows, width), bf16),
                pltpu.VMEM((STRIP // FINE, rows), f32), pltpu.VMEM((STRIP // FINE, rows), f32),
                pltpu.VMEM((FINE, rows), f32), pltpu.VMEM((FINE, rows), f32),
                pltpu.VMEM((width // FINE, lanes), f32), pltpu.VMEM((width // FINE, lanes), f32),
                pltpu.VMEM((cols, 2 * STRIP, rows), bf16),
                pltpu.VMEM((2 * width, lanes), bf16), pltpu.VMEM((2 * width, lanes), bf16),
                pltpu.VMEM((highs, *part), bf16), pltpu.VMEM((highs, *part), bf16),
                pltpu.VMEM((far, *part), f32),
                pltpu.VMEM((far, *part), bf16), pltpu.VMEM((far, *part), bf16),
                pltpu.VMEM(part, f32),
                pltpu.VMEM(part, bf16), pltpu.VMEM(part, bf16),
                pltpu.VMEM((2 * STRIP, lanes), f32),
                pltpu.VMEM(slot, f32),
                pltpu.VMEM((zs - 1, *slot), bf16), pltpu.VMEM((zs - 1, *slot), bf16),
                sem((5,)), sem((PIECES,)),
                sem((highs, CHUNKS)), sem((highs, CHUNKS)),
                sem((far, CHUNKS)), sem((far, CHUNKS)),
                sem((CHUNKS,)), sem((CHUNKS,)),
                sem((zs - 1, CHUNKS)), sem((zs - 1, CHUNKS)),
            ],
            compiler_params=pltpu.CompilerParams(
                collective_id=0, has_side_effects=True, vmem_limit_bytes=32 * 1024 * 1024),
        )(*[pltpu.with_memory_space_constraint(value, pltpu.HBM) for value in (
            row_offset, column_offset, slot_subgrid, row_taper.reshape(1, -1), column_taper.reshape(1, -1), facets)])
        grid = pl.pallas_call(
            place_kernel,
            out_shape=jax.ShapeDtypeStruct((2, SUBGRID, STRIP), f32),
            in_specs=[pl.BlockSpec(memory_space=pltpu.SMEM), pl.BlockSpec(memory_space=pltpu.VMEM)],
            out_specs=pl.BlockSpec(memory_space=pltpu.HBM),
            scratch_shapes=[pltpu.VMEM((2, SUBGRID + STRIP + 8, STRIP), f32), sem((2,))],
            compiler_params=pltpu.CompilerParams(vmem_limit_bytes=8 * 1024 * 1024),
        )(column_place, grid)
        return grid.reshape(1, 1, 2, SUBGRID, STRIP)

    in_specs = (P(None, "col", "fac"), P("col"), P(), P(), P(), P(), P())
    out_specs = P("col", "fac", None, None, None)
    return jax.shard_map(on_device, mesh=mesh, in_specs=in_specs, out_specs=out_specs, check_vma=False)
```

```python
import functools
import math

import jax
import jax.numpy as jnp
from jax import lax
from jax.experimental import pallas as pl
from jax.experimental.pallas import tpu as pltpu
from jax.sharding import PartitionSpec as P

FACET = 4096
STRIP = 128
SUBGRID = 512
FINE = 16
SIZES = (16, 16, 16, 16, 16, 16, 16, 16)
CHUNKS = len(SIZES)
HOP_ROWS = 68
HALVES = 2
HALF = STRIP // HALVES
MESH = pl.DeviceIdType.MESH


def unit_phase(phases):
    quarter = FACET // 4
    shifted = phases + quarter // 2
    angle = ((shifted & (quarter - 1)) - quarter // 2).astype(jnp.float32) * (2.0 * math.pi / FACET)
    turn = lax.shift_right_logical(shifted & (FACET - 1), quarter.bit_length() - 1)
    sq = angle * angle
    cosine = 1.0 + sq * (-1 / 2 + sq * (1 / 24 + sq * (-1 / 720 + sq * (1 / 40320))))
    sine = angle * (1.0 + sq * (-1 / 6 + sq * (1 / 120 + sq * (-1 / 5040 + sq * (1 / 362880)))))
    odd = (turn & 1) == 1
    first = jnp.where(odd, sine, cosine)
    second = jnp.where(odd, cosine, sine)
    real = jnp.where(((turn + 1) & 2) == 2, -first, first)
    imag = jnp.where((turn & 2) == 2, second, -second)
    return real, imag


def span(j):
    start = 2 * sum(SIZES[:j])
    return slice(start, start + 2 * SIZES[j])


def order():
    far_done, free, events = 0, 0, []
    for j, size in enumerate(SIZES):
        far_done += size
        free = max(free, far_done) + size
        events += [(far_done, 0, j), (free + HOP_ROWS, 1, j)]
    return [event[1:] for event in sorted(events)]


def chunks_of(half):
    return [j for j in range(CHUNKS) if sum(SIZES[:j]) // HALF == half]


def iota(shape, dim):
    return lax.broadcasted_iota(jnp.int32, shape, dim)


def kernel(
    cols, facs,
    row_offset_in, column_offset_in, slot_subgrid_in, row_taper_in, column_taper_in, facets,
    out,
    row_offset, column_offset, slot_subgrid, row_taper, column_gain, held, coarse_r, coarse_i, fine_r, fine_i, steep_r, steep_i, encode, decode_r, decode_i,
    pair_out, pair_in, far_part, far_out, far_in, own_part, strip, strip_in,
    partial, mine, sums, slots_out, slots_in,
    small_sem, held_sem, pair_send, pair_recv, far_send, far_recv, strip_send, strip_recv, slot_send, slot_recv,
):
    col = lax.axis_index("col")
    fac = lax.axis_index("fac")
    col_hi, core = col // 2, col % 2
    fac_hi, fac_lo = fac // 2, fac % 2
    highs, zs = cols // 2, facs // 2
    rows, width = facets.shape[1], facets.shape[2]

    pair_id = (col_hi * 2 + 1 - core, fac)
    far_ids = [((col_hi + d) % highs * 2 + core, fac) for d in range(1, highs)]
    strip_id = (col, fac_hi * 2 + 1 - fac_lo)
    slot_ids = [(col, (fac_hi + d) % zs * 2 + fac_lo) for d in range(1, zs)]
    peers = [pair_id, *far_ids, strip_id, *slot_ids]
    own_columns = pl.ds(pl.multiple_of(fac * width, width), width)
    small = [
        pltpu.make_async_copy(source, target, small_sem.at[n])
        for n, (source, target) in enumerate((
            (row_offset_in, row_offset), (column_offset_in, column_offset), (slot_subgrid_in, slot_subgrid),
            (row_taper_in, row_taper),
            (column_taper_in.at[:, own_columns], column_gain)))]
    loads = [pltpu.make_async_copy(facets.at[p], held.at[p], held_sem.at[p]) for p in range(2)]
    for load in (*small, *loads):
        load.start()
    barrier = pltpu.get_barrier_semaphore()
    for peer in peers:
        pl.semaphore_signal(barrier, inc=1, device_id=peer, device_id_type=MESH)

    steps = STRIP // FINE
    position = col * rows + iota((1, rows), 1)
    fine_r[...], fine_i[...] = unit_phase(iota((FINE, rows), 0) * position)
    for load in small:
        load.wait()
    gain = row_taper[...] * (1.0 / math.sqrt(FACET))

    def coarse(own, group):
        first = (row_offset[group] + FINE * iota((steps, rows), 0)) & (FACET - 1)
        real, imag = unit_phase(first * position)
        coarse_r[own] = real * gain
        coarse_i[own] = imag * gain

    def encode_half(index, own, half):
        def row(i, carry):
            source = pl.ds(half * (steps // HALVES) + i, 1)
            ar, ai = coarse_r[own, source, :], coarse_i[own, source, :]
            br, bi = fine_r[...], fine_i[...]
            at = pl.multiple_of(i * FINE, FINE) + half * 2 * HALF
            encode[index, pl.ds(at, FINE), :] = (ar * br - ai * bi).astype(jnp.bfloat16)
            encode[index, pl.ds(at + HALF, FINE), :] = (ar * bi + ai * br).astype(jnp.bfloat16)
            return carry

        lax.fori_loop(0, steps // HALVES, row, 0)

    def product(target, index, halves):
        table = encode[index, halves[0] * 2 * HALF:(halves[-1] + 1) * 2 * HALF]
        by_real, by_imag = [jnp.dot(table, held[p], preferred_element_type=jnp.float32) for p in range(2)]
        for n, half in enumerate(halves):
            at = n * 2 * HALF
            real = by_real[at:at + HALF] - by_imag[at + HALF:at + 2 * HALF]
            imag = by_imag[at:at + HALF] + by_real[at + HALF:at + 2 * HALF]
            for j in chunks_of(half):
                begin, size = span(j).start, SIZES[j]
                first = begin // 2 - half * HALF
                target[begin:begin + size] = real[first:first + size].astype(target.dtype)
                target[begin + size:begin + 2 * size] = imag[first:first + size].astype(target.dtype)

    def sends(source, target, send, recv, peer):
        return pltpu.make_async_remote_copy(
            src_ref=source, dst_ref=target, send_sem=send, recv_sem=recv, device_id=peer, device_id_type=MESH)

    def pair_copy(d, half):
        at = pl.ds(half * 2 * HALF, 2 * HALF)
        return sends(pair_out.at[d, at], pair_in.at[d, at], pair_send.at[0], pair_recv.at[d, half], pair_id)

    def far_copy(d, j):
        return sends(
            far_out.at[d - 1, span(j)], far_in.at[d - 1, span(j)], far_send.at[0], far_recv.at[d - 1, j], far_ids[d - 1])

    def strip_copy(j):
        return sends(strip.at[span(j)], strip_in.at[span(j)], strip_send.at[0], strip_recv.at[j], strip_id)

    def slot_copy(d, j):
        return sends(
            slots_out.at[d - 1, span(j)], slots_in.at[d - 1, span(j)], slot_send.at[0], slot_recv.at[j], slot_ids[d - 1])

    def slots_at(j):
        return sends(slots_out.at[:, span(j)], slots_in.at[:, span(j)], slot_send.at[0], slot_recv.at[j], strip_id)

    whole = range(HALVES)

    def group_of(d, own):
        return (col_hi + d) % highs * 2 + (core if own else 1 - core)

    def relay(d, half):
        pair_copy(d, half).wait_recv()
        for j in chunks_of(half):
            far_out[d - 1, span(j)] = (
                far_part[d - 1, span(j)] + pair_in[d, span(j)].astype(jnp.float32)).astype(jnp.bfloat16)
            far_copy(d, j).start()

    def send_pair(d, halves):
        for half in halves:
            pair_copy(d, half).start()

    for d in range(1, highs):
        for own in range(2):
            coarse(own, group_of(d, own))
            encode_half(2 * d + own, own, 0)
        if d == 1:
            for load in loads:
                load.wait()
        product(pair_out.at[d], 2 * d, [0])
        if d == 1:
            pl.semaphore_wait(barrier, len(peers))
        send_pair(d, [0])
        product(far_part.at[d - 1], 2 * d + 1, [0])
        for own in range(2):
            for half in whole[1:]:
                encode_half(2 * d + own, own, half)
        for half in whole[1:]:
            product(pair_out.at[d], 2 * d, [half])
            send_pair(d, [half])
        relay(d, 0)
        for half in whole[1:]:
            product(far_part.at[d - 1], 2 * d + 1, [half])
    for own in range(2):
        coarse(own, group_of(0, own))
        for half in whole:
            encode_half(own, own, half)
        if own == 0:
            product(pair_out.at[0], 0, whole)
            send_pair(0, whole)
            for d in range(1, highs):
                for half in whole[1:]:
                    relay(d, half)
    product(own_part, 1, whole)

    def decoded(block, part):
        at = slice(part * width, (part + 1) * width)
        size = block.shape[0] // 2
        by_real = jnp.dot(block, decode_r[at], preferred_element_type=jnp.float32)
        by_imag = jnp.dot(block, decode_i[at], preferred_element_type=jnp.float32)
        return jnp.concatenate([by_real[:size] - by_imag[size:], by_imag[:size] + by_real[size:]], axis=0)

    def arrive(j):
        if j in [chunks_of(half)[0] for half in whole]:
            pair_copy(0, span(j).start // (2 * HALF)).wait_recv()
        total = own_part[span(j)] + pair_in[0, span(j)].astype(jnp.float32)
        for d in range(1, highs):
            far_copy(d, j).wait_recv()
            total = total + far_in[d - 1, span(j)].astype(jnp.float32)
        strip[span(j)] = (total * column_gain[...]).astype(jnp.bfloat16)
        strip_copy(j).start()

    def finish(j):
        strip_copy(j).wait_recv()
        total = partial[span(j)] + decoded(strip_in[span(j)], 1)
        mine[span(j)] = total[:, :STRIP]
        for d in range(1, zs):
            slots_out[d - 1, span(j)] = total[:, d * STRIP:(d + 1) * STRIP].astype(jnp.bfloat16)
            slot_copy(d, j).start()

    lanes = zs * STRIP
    coarse_n = width // FINE
    starts = []
    for d in range(zs):
        start = column_offset[slot_subgrid[col, (fac_hi + d) % zs * 2 + fac_lo]]
        starts.append((start + iota((1, STRIP), 1)) & (FACET - 1))
    frequency = jnp.concatenate(starts, axis=1)
    fine_real, fine_imag = unit_phase(iota((FINE, lanes), 0) * frequency)
    fine_real, fine_imag = fine_real * (1.0 / math.sqrt(FACET)), fine_imag * (1.0 / math.sqrt(FACET))
    for part, block in enumerate((fac, fac_hi * 2 + 1 - fac_lo)):
        base = part * width
        steep_r[...], steep_i[...] = unit_phase((block * width + FINE * iota((coarse_n, lanes), 0)) * frequency)

        def row(i, carry, base=base):
            ar, ai = steep_r[pl.ds(i, 1), :], steep_i[pl.ds(i, 1), :]
            at = pl.multiple_of(base + i * FINE, FINE)
            decode_r[pl.ds(at, FINE), :] = (ar * fine_real - ai * fine_imag).astype(jnp.bfloat16)
            decode_i[pl.ds(at, FINE), :] = (ar * fine_imag + ai * fine_real).astype(jnp.bfloat16)
            return carry

        lax.fori_loop(0, coarse_n, row, 0)

    for stage, j in order():
        if stage == 0:
            arrive(j)
            partial[span(j)] = decoded(strip[span(j)], 0)
        else:
            finish(j)

    sends(pair_out, pair_in, pair_send.at[0], pair_recv.at[0, 0], pair_id).wait_send()
    if highs > 1:
        sends(far_out, far_in, far_send.at[0], far_recv.at[0, 0], far_ids[0]).wait_send()
    sends(strip, strip_in, strip_send.at[0], strip_recv.at[0], strip_id).wait_send()
    for j, size in enumerate(SIZES):
        total = mine[span(j)]
        slots_at(j).wait_recv()
        for d in range(1, zs):
            total = total + slots_in[d - 1, span(j)].astype(jnp.float32)
        first = span(j).start // 2
        for p in range(2):
            sums[p, first:first + size] = total[p * size:(p + 1) * size]
    for p in range(2):
        out[p] = sums[p].T
    sends(slots_out, slots_in, slot_send.at[0], slot_recv.at[0], strip_id).wait_send()


def place_kernel(place, part, out, grid, sem):
    shift = lax.rem(place[0], 8)
    first = pl.multiple_of(place[0] - shift, 8)
    band = STRIP + 8
    copies = [pltpu.make_async_copy(grid.at[n, pl.ds(0, SUBGRID)], out.at[n], sem.at[n]) for n in range(2)]
    for n in range(2):
        grid[n] = jnp.zeros(grid.shape[1:], jnp.float32)
        grid[n, pl.ds(first, band)] = pltpu.roll(
            jnp.concatenate([part[n], jnp.zeros((8, STRIP), jnp.float32)], axis=0), shift, 0)
        grid[n, :band] += grid[n, SUBGRID:]
        copies[n].start()
    for copy in copies:
        copy.wait()


def solution(mesh):
    cols, facs = mesh.shape["col"], mesh.shape["fac"]
    highs, zs = cols // 2, facs // 2

    def on_device(facets, row_taper, column_taper, column_place, row_offset, column_offset, slot_subgrid):
        rows, width = facets.shape[1], facets.shape[2]
        bf16, f32 = jnp.bfloat16, jnp.float32
        lanes = zs * STRIP
        part = (2 * STRIP, width)
        slot = (2 * STRIP, STRIP)
        far = max(highs - 1, 1)
        sem = pltpu.SemaphoreType.DMA
        grid = pl.pallas_call(
            functools.partial(kernel, cols, facs),
            out_shape=jax.ShapeDtypeStruct((2, STRIP, STRIP), f32),
            in_specs=[pl.BlockSpec(memory_space=pltpu.HBM)] * 6,
            out_specs=pl.BlockSpec(memory_space=pltpu.VMEM),
            scratch_shapes=[
                pltpu.SMEM(row_offset.shape, jnp.int32), pltpu.SMEM(column_offset.shape, jnp.int32),
                pltpu.SMEM(slot_subgrid.shape, jnp.int32),
                pltpu.VMEM((1, rows), f32), pltpu.VMEM((1, width), f32),
                pltpu.VMEM((2, rows, width), bf16),
                pltpu.VMEM((2, STRIP // FINE, rows), f32), pltpu.VMEM((2, STRIP // FINE, rows), f32),
                pltpu.VMEM((FINE, rows), f32), pltpu.VMEM((FINE, rows), f32),
                pltpu.VMEM((width // FINE, lanes), f32), pltpu.VMEM((width // FINE, lanes), f32),
                pltpu.VMEM((cols, 2 * STRIP, rows), bf16),
                pltpu.VMEM((2 * width, lanes), bf16), pltpu.VMEM((2 * width, lanes), bf16),
                pltpu.VMEM((highs, *part), bf16), pltpu.VMEM((highs, *part), bf16),
                pltpu.VMEM((far, *part), f32),
                pltpu.VMEM((far, *part), bf16), pltpu.VMEM((far, *part), bf16),
                pltpu.VMEM(part, f32),
                pltpu.VMEM(part, bf16), pltpu.VMEM(part, bf16),
                pltpu.VMEM((2 * STRIP, lanes), f32),
                pltpu.VMEM(slot, f32), pltpu.VMEM((2, STRIP, STRIP), f32),
                pltpu.VMEM((zs - 1, *slot), bf16), pltpu.VMEM((zs - 1, *slot), bf16),
                sem((5,)), sem((2,)),
                sem((1,)), sem((highs, HALVES)),
                sem((1,)), sem((far, CHUNKS)),
                sem((1,)), sem((CHUNKS,)),
                sem((1,)), sem((CHUNKS,)),
            ],
            compiler_params=pltpu.CompilerParams(
                collective_id=0, has_side_effects=True, vmem_limit_bytes=32 * 1024 * 1024),
        )(*[pltpu.with_memory_space_constraint(value, pltpu.HBM) for value in (
            row_offset, column_offset, slot_subgrid, row_taper.reshape(1, -1), column_taper.reshape(1, -1), facets)])
        grid = pl.pallas_call(
            place_kernel,
            out_shape=jax.ShapeDtypeStruct((2, SUBGRID, STRIP), f32),
            in_specs=[pl.BlockSpec(memory_space=pltpu.SMEM), pl.BlockSpec(memory_space=pltpu.VMEM)],
            out_specs=pl.BlockSpec(memory_space=pltpu.HBM),
            scratch_shapes=[pltpu.VMEM((2, SUBGRID + STRIP + 8, STRIP), f32), sem((2,))],
            compiler_params=pltpu.CompilerParams(vmem_limit_bytes=8 * 1024 * 1024),
        )(column_place, grid)
        return grid.reshape(1, 1, 2, SUBGRID, STRIP)

    in_specs = (P(None, "col", "fac"), P("col"), P(), P(), P(), P(), P())
    out_specs = P("col", "fac", None, None, None)
    return jax.shard_map(on_device, mesh=mesh, in_specs=in_specs, out_specs=out_specs, check_vma=False)
```

```python
import functools
import math

import jax
import jax.numpy as jnp
from jax import lax
from jax.experimental import pallas as pl
from jax.experimental.pallas import tpu as pltpu
from jax.sharding import PartitionSpec as P

FACET = 4096
STRIP = 128
SUBGRID = 512
FINE = 16
SIZES = (16, 16, 16, 16, 16, 16, 16, 16)
CHUNKS = len(SIZES)
HOP_ROWS = 68
HALVES = 2
HALF = STRIP // HALVES
MESH = pl.DeviceIdType.MESH


def unit_phase(phases):
    quarter = FACET // 4
    shifted = phases + quarter // 2
    angle = ((shifted & (quarter - 1)) - quarter // 2).astype(jnp.float32) * (2.0 * math.pi / FACET)
    turn = lax.shift_right_logical(shifted & (FACET - 1), quarter.bit_length() - 1)
    sq = angle * angle
    cosine = 1.0 + sq * (-1 / 2 + sq * (1 / 24 + sq * (-1 / 720 + sq * (1 / 40320))))
    sine = angle * (1.0 + sq * (-1 / 6 + sq * (1 / 120 + sq * (-1 / 5040 + sq * (1 / 362880)))))
    odd = (turn & 1) == 1
    first = jnp.where(odd, sine, cosine)
    second = jnp.where(odd, cosine, sine)
    real = jnp.where(((turn + 1) & 2) == 2, -first, first)
    imag = jnp.where((turn & 2) == 2, second, -second)
    return real, imag


def span(j):
    start = 2 * sum(SIZES[:j])
    return slice(start, start + 2 * SIZES[j])


def order():
    far_done, free, events = 0, 0, []
    for j, size in enumerate(SIZES):
        far_done += size
        free = max(free, far_done) + size
        events += [(far_done, 0, j), (free + HOP_ROWS, 1, j)]
    return [event[1:] for event in sorted(events)]


def chunks_of(half):
    return [j for j in range(CHUNKS) if sum(SIZES[:j]) // HALF == half]


def iota(shape, dim):
    return lax.broadcasted_iota(jnp.int32, shape, dim)


def kernel(
    cols, facs,
    row_offset_in, column_offset_in, slot_subgrid_in, row_taper_in, column_taper_in, facets,
    out,
    row_offset, column_offset, slot_subgrid, row_taper, column_gain, held, coarse_r, coarse_i, fine_r, fine_i, steep_r, steep_i, encode, decode_r, decode_i,
    pair_out, pair_in, far_part, far_out, far_in, own_part, strip, strip_in,
    partial, mine, sums, slots_out, slots_in,
    small_sem, held_sem, pair_send, pair_recv, far_send, far_recv, strip_send, strip_recv, slot_send, slot_recv,
):
    col = lax.axis_index("col")
    fac = lax.axis_index("fac")
    col_hi, core = col // 2, col % 2
    fac_hi, fac_lo = fac // 2, fac % 2
    highs, zs = cols // 2, facs // 2
    rows, width = facets.shape[1], facets.shape[2]

    pair_id = (col_hi * 2 + 1 - core, fac)
    far_ids = [((col_hi + d) % highs * 2 + core, fac) for d in range(1, highs)]
    strip_id = (col, fac_hi * 2 + 1 - fac_lo)
    slot_ids = [(col, (fac_hi + d) % zs * 2 + fac_lo) for d in range(1, zs)]
    peers = [pair_id, *far_ids, strip_id, *slot_ids]
    own_columns = pl.ds(pl.multiple_of(fac * width, width), width)
    small = [
        pltpu.make_async_copy(source, target, small_sem.at[n])
        for n, (source, target) in enumerate((
            (row_offset_in, row_offset), (column_offset_in, column_offset), (slot_subgrid_in, slot_subgrid),
            (row_taper_in, row_taper),
            (column_taper_in.at[:, own_columns], column_gain)))]
    loads = [pltpu.make_async_copy(facets.at[p], held.at[p], held_sem.at[p]) for p in range(2)]
    for load in (*small, *loads):
        load.start()
    barrier = pltpu.get_barrier_semaphore()
    for peer in peers:
        pl.semaphore_signal(barrier, inc=1, device_id=peer, device_id_type=MESH)

    steps = STRIP // FINE
    position = col * rows + iota((1, rows), 1)
    fine_r[...], fine_i[...] = unit_phase(iota((FINE, rows), 0) * position)
    for load in small:
        load.wait()
    gain = row_taper[...] * (1.0 / math.sqrt(FACET))

    def coarse(own, group):
        first = (row_offset[group] + FINE * iota((steps, rows), 0)) & (FACET - 1)
        real, imag = unit_phase(first * position)
        coarse_r[own] = real * gain
        coarse_i[own] = imag * gain

    def encode_half(index, own, half):
        def row(i, carry):
            source = pl.ds(half * (steps // HALVES) + i, 1)
            ar, ai = coarse_r[own, source, :], coarse_i[own, source, :]
            br, bi = fine_r[...], fine_i[...]
            at = pl.multiple_of(i * FINE, FINE) + half * 2 * HALF
            encode[index, pl.ds(at, FINE), :] = (ar * br - ai * bi).astype(jnp.bfloat16)
            encode[index, pl.ds(at + HALF, FINE), :] = (ar * bi + ai * br).astype(jnp.bfloat16)
            return carry

        lax.fori_loop(0, steps // HALVES, row, 0)

    def product(target, index, halves):
        table = encode[index, halves[0] * 2 * HALF:(halves[-1] + 1) * 2 * HALF]
        by_real, by_imag = [jnp.dot(table, held[p], preferred_element_type=jnp.float32) for p in range(2)]
        for n, half in enumerate(halves):
            at = n * 2 * HALF
            real = by_real[at:at + HALF] - by_imag[at + HALF:at + 2 * HALF]
            imag = by_imag[at:at + HALF] + by_real[at + HALF:at + 2 * HALF]
            for j in chunks_of(half):
                begin, size = span(j).start, SIZES[j]
                first = begin // 2 - half * HALF
                target[begin:begin + size] = real[first:first + size].astype(target.dtype)
                target[begin + size:begin + 2 * size] = imag[first:first + size].astype(target.dtype)

    def sends(source, target, send, recv, peer):
        return pltpu.make_async_remote_copy(
            src_ref=source, dst_ref=target, send_sem=send, recv_sem=recv, device_id=peer, device_id_type=MESH)

    def pair_copy(d, half):
        at = pl.ds(half * 2 * HALF, 2 * HALF)
        return sends(pair_out.at[d, at], pair_in.at[d, at], pair_send.at[0], pair_recv.at[d, half], pair_id)

    def far_copy(d, j):
        return sends(
            far_out.at[d - 1, span(j)], far_in.at[d - 1, span(j)], far_send.at[0], far_recv.at[d - 1, j], far_ids[d - 1])

    def strip_copy(j):
        return sends(strip.at[span(j)], strip_in.at[span(j)], strip_send.at[0], strip_recv.at[j], strip_id)

    def slot_copy(d, j):
        return sends(
            slots_out.at[d - 1, span(j)], slots_in.at[d - 1, span(j)], slot_send.at[0], slot_recv.at[j // (CHUNKS - 1)], slot_ids[d - 1])

    def slots_wait(last):
        edge = span(CHUNKS - 1).start
        at = slice(edge, 2 * STRIP) if last else slice(0, edge)
        sends(slots_out.at[:, at], slots_in.at[:, at], slot_send.at[0], slot_recv.at[last], strip_id).wait_recv()

    whole = range(HALVES)

    def group_of(d, own):
        return (col_hi + d) % highs * 2 + (core if own else 1 - core)

    def relay(d, half):
        pair_copy(d, half).wait_recv()
        for j in chunks_of(half):
            far_out[d - 1, span(j)] = (
                far_part[d - 1, span(j)] + pair_in[d, span(j)].astype(jnp.float32)).astype(jnp.bfloat16)
            far_copy(d, j).start()

    def send_pair(d, halves):
        for half in halves:
            pair_copy(d, half).start()

    for d in range(1, highs):
        coarse(0, group_of(d, 0))
        encode_half(2 * d, 0, 0)
        if d == 1:
            for load in loads:
                load.wait()
        product(pair_out.at[d], 2 * d, [0])
        if d == 1:
            pl.semaphore_wait(barrier, len(peers))
        send_pair(d, [0])
        coarse(1, group_of(d, 1))
        encode_half(2 * d + 1, 1, 0)
        product(far_part.at[d - 1], 2 * d + 1, [0])
        for own in range(2):
            for half in whole[1:]:
                encode_half(2 * d + own, own, half)
        relay(d, 0)
        for half in whole[1:]:
            product(pair_out.at[d], 2 * d, [half])
            send_pair(d, [half])
        for half in whole[1:]:
            product(far_part.at[d - 1], 2 * d + 1, [half])
    for own in range(2):
        coarse(own, group_of(0, own))
        for half in whole:
            encode_half(own, own, half)
        if own == 0:
            product(pair_out.at[0], 0, whole)
            send_pair(0, whole)
            for d in range(1, highs):
                for half in whole[1:]:
                    relay(d, half)
    product(own_part, 1, whole)

    def decoded(block):
        size = block.shape[0] // 2
        by_real = jnp.dot(block, decode_r[...], preferred_element_type=jnp.float32)
        by_imag = jnp.dot(block, decode_i[...], preferred_element_type=jnp.float32)
        return by_real[:size] - by_imag[size:], by_imag[:size] + by_real[size:]

    def arrive(j):
        if j in [chunks_of(half)[0] for half in whole]:
            pair_copy(0, span(j).start // (2 * HALF)).wait_recv()
        total = own_part[span(j)] + pair_in[0, span(j)].astype(jnp.float32)
        for d in range(1, highs):
            far_copy(d, j).wait_recv()
            total = total + far_in[d - 1, span(j)].astype(jnp.float32)
        strip[span(j)] = (total * column_gain[...]).astype(jnp.bfloat16)
        strip_copy(j).start()

    def finish(j):
        strip_copy(j).wait_recv()
        real, imag = decoded(strip_in[span(j)])
        total = partial[span(j)] + jnp.concatenate(
            [real * shift_real - imag * shift_imag, imag * shift_real + real * shift_imag], axis=0)
        mine[span(j)] = total[:, :STRIP]
        for d in range(1, zs):
            slots_out[d - 1, span(j)] = total[:, d * STRIP:(d + 1) * STRIP].astype(jnp.bfloat16)
            slot_copy(d, j).start()

    lanes = zs * STRIP
    coarse_n = width // FINE
    starts = []
    for d in range(zs):
        start = column_offset[slot_subgrid[col, (fac_hi + d) % zs * 2 + fac_lo]]
        starts.append((start + iota((1, STRIP), 1)) & (FACET - 1))
    frequency = jnp.concatenate(starts, axis=1)
    fine_real, fine_imag = unit_phase(iota((FINE, lanes), 0) * frequency)
    fine_real, fine_imag = fine_real * (1.0 / math.sqrt(FACET)), fine_imag * (1.0 / math.sqrt(FACET))
    steep_r[...], steep_i[...] = unit_phase((fac * width + FINE * iota((coarse_n, lanes), 0)) * frequency)
    shift_real, shift_imag = unit_phase((1 - 2 * fac_lo) * width * frequency)

    def row(i, carry):
        ar, ai = steep_r[pl.ds(i, 1), :], steep_i[pl.ds(i, 1), :]
        at = pl.multiple_of(i * FINE, FINE)
        decode_r[pl.ds(at, FINE), :] = (ar * fine_real - ai * fine_imag).astype(jnp.bfloat16)
        decode_i[pl.ds(at, FINE), :] = (ar * fine_imag + ai * fine_real).astype(jnp.bfloat16)
        return carry

    lax.fori_loop(0, coarse_n, row, 0)

    for stage, j in order():
        if stage == 0:
            arrive(j)
            partial[span(j)] = jnp.concatenate(decoded(strip[span(j)]), axis=0)
        else:
            finish(j)

    sends(pair_out, pair_in, pair_send.at[0], pair_recv.at[0, 0], pair_id).wait_send()
    if highs > 1:
        sends(far_out, far_in, far_send.at[0], far_recv.at[0, 0], far_ids[0]).wait_send()
    sends(strip, strip_in, strip_send.at[0], strip_recv.at[0], strip_id).wait_send()
    for j, size in enumerate(SIZES):
        total = mine[span(j)]
        if j in (0, CHUNKS - 1):
            slots_wait(j // (CHUNKS - 1))
        for d in range(1, zs):
            total = total + slots_in[d - 1, span(j)].astype(jnp.float32)
        first = span(j).start // 2
        for p in range(2):
            sums[p, first:first + size] = total[p * size:(p + 1) * size]
    for p in range(2):
        out[p] = sums[p].T
    sends(slots_out, slots_in, slot_send.at[0], slot_recv.at[0], strip_id).wait_send()


def place_kernel(place, part, out, grid, sem):
    shift = lax.rem(place[0], 8)
    first = pl.multiple_of(place[0] - shift, 8)
    band = STRIP + 8
    copies = [pltpu.make_async_copy(grid.at[n, pl.ds(0, SUBGRID)], out.at[n], sem.at[n]) for n in range(2)]
    for n in range(2):
        grid[n] = jnp.zeros(grid.shape[1:], jnp.float32)
        grid[n, pl.ds(first, band)] = pltpu.roll(
            jnp.concatenate([part[n], jnp.zeros((8, STRIP), jnp.float32)], axis=0), shift, 0)
        grid[n, :band] += grid[n, SUBGRID:]
        copies[n].start()
    for copy in copies:
        copy.wait()


def solution(mesh):
    cols, facs = mesh.shape["col"], mesh.shape["fac"]
    highs, zs = cols // 2, facs // 2

    def on_device(facets, row_taper, column_taper, column_place, row_offset, column_offset, slot_subgrid):
        rows, width = facets.shape[1], facets.shape[2]
        bf16, f32 = jnp.bfloat16, jnp.float32
        lanes = zs * STRIP
        part = (2 * STRIP, width)
        slot = (2 * STRIP, STRIP)
        far = max(highs - 1, 1)
        sem = pltpu.SemaphoreType.DMA
        grid = pl.pallas_call(
            functools.partial(kernel, cols, facs),
            out_shape=jax.ShapeDtypeStruct((2, STRIP, STRIP), f32),
            in_specs=[pl.BlockSpec(memory_space=pltpu.HBM)] * 6,
            out_specs=pl.BlockSpec(memory_space=pltpu.VMEM),
            scratch_shapes=[
                pltpu.SMEM(row_offset.shape, jnp.int32), pltpu.SMEM(column_offset.shape, jnp.int32),
                pltpu.SMEM(slot_subgrid.shape, jnp.int32),
                pltpu.VMEM((1, rows), f32), pltpu.VMEM((1, width), f32),
                pltpu.VMEM((2, rows, width), bf16),
                pltpu.VMEM((2, STRIP // FINE, rows), f32), pltpu.VMEM((2, STRIP // FINE, rows), f32),
                pltpu.VMEM((FINE, rows), f32), pltpu.VMEM((FINE, rows), f32),
                pltpu.VMEM((width // FINE, lanes), f32), pltpu.VMEM((width // FINE, lanes), f32),
                pltpu.VMEM((cols, 2 * STRIP, rows), bf16),
                pltpu.VMEM((width, lanes), bf16), pltpu.VMEM((width, lanes), bf16),
                pltpu.VMEM((highs, *part), bf16), pltpu.VMEM((highs, *part), bf16),
                pltpu.VMEM((far, *part), f32),
                pltpu.VMEM((far, *part), bf16), pltpu.VMEM((far, *part), bf16),
                pltpu.VMEM(part, f32),
                pltpu.VMEM(part, bf16), pltpu.VMEM(part, bf16),
                pltpu.VMEM((2 * STRIP, lanes), f32),
                pltpu.VMEM(slot, f32), pltpu.VMEM((2, STRIP, STRIP), f32),
                pltpu.VMEM((zs - 1, *slot), bf16), pltpu.VMEM((zs - 1, *slot), bf16),
                sem((5,)), sem((2,)),
                sem((1,)), sem((highs, HALVES)),
                sem((1,)), sem((far, CHUNKS)),
                sem((1,)), sem((CHUNKS,)),
                sem((1,)), sem((2,)),
            ],
            compiler_params=pltpu.CompilerParams(
                collective_id=0, has_side_effects=True, vmem_limit_bytes=32 * 1024 * 1024),
        )(*[pltpu.with_memory_space_constraint(value, pltpu.HBM) for value in (
            row_offset, column_offset, slot_subgrid, row_taper.reshape(1, -1), column_taper.reshape(1, -1), facets)])
        grid = pl.pallas_call(
            place_kernel,
            out_shape=jax.ShapeDtypeStruct((2, SUBGRID, STRIP), f32),
            in_specs=[pl.BlockSpec(memory_space=pltpu.SMEM), pl.BlockSpec(memory_space=pltpu.VMEM)],
            out_specs=pl.BlockSpec(memory_space=pltpu.HBM),
            scratch_shapes=[pltpu.VMEM((2, SUBGRID + STRIP + 8, STRIP), f32), sem((2,))],
            compiler_params=pltpu.CompilerParams(vmem_limit_bytes=8 * 1024 * 1024),
        )(column_place, grid)
        return grid.reshape(1, 1, 2, SUBGRID, STRIP)

    in_specs = (P(None, "col", "fac"), P("col"), P(), P(), P(), P(), P())
    out_specs = P("col", "fac", None, None, None)
    return jax.shard_map(on_device, mesh=mesh, in_specs=in_specs, out_specs=out_specs, check_vma=False)
```

```python
import functools
import math

import jax
import jax.numpy as jnp
from jax import lax
from jax.experimental import pallas as pl
from jax.experimental.pallas import tpu as pltpu
from jax.sharding import PartitionSpec as P

FACET = 4096
STRIP = 128
SUBGRID = 512
FINE = 16
SIZES = (16, 16, 16, 16, 16, 16, 16, 16)
CHUNKS = len(SIZES)
HOP_ROWS = 68
LEAD = 2
HALVES = 2
HALF = STRIP // HALVES
MESH = pl.DeviceIdType.MESH


def unit_phase(phases):
    quarter = FACET // 4
    shifted = phases + quarter // 2
    angle = ((shifted & (quarter - 1)) - quarter // 2).astype(jnp.float32) * (2.0 * math.pi / FACET)
    turn = lax.shift_right_logical(shifted & (FACET - 1), quarter.bit_length() - 1)
    sq = angle * angle
    cosine = 1.0 + sq * (-1 / 2 + sq * (1 / 24 + sq * (-1 / 720 + sq * (1 / 40320))))
    sine = angle * (1.0 + sq * (-1 / 6 + sq * (1 / 120 + sq * (-1 / 5040 + sq * (1 / 362880)))))
    odd = (turn & 1) == 1
    first = jnp.where(odd, sine, cosine)
    second = jnp.where(odd, cosine, sine)
    real = jnp.where(((turn + 1) & 2) == 2, -first, first)
    imag = jnp.where((turn & 2) == 2, second, -second)
    return real, imag


def span(j):
    start = 2 * sum(SIZES[:j])
    return slice(start, start + 2 * SIZES[j])


def order():
    far_done, free, events = 0, 0, []
    for j, size in enumerate(SIZES):
        far_done += size
        free = max(free, far_done) + size
        events += [(far_done, 0, j), (free + HOP_ROWS, 1, j)]
    return [event[1:] for event in sorted(events)]


def chunks_of(half):
    return [j for j in range(CHUNKS) if sum(SIZES[:j]) // HALF == half]


def iota(shape, dim):
    return lax.broadcasted_iota(jnp.int32, shape, dim)


def kernel(
    cols, facs,
    row_offset_in, column_offset_in, slot_subgrid_in, row_taper_in, column_taper_in, facets,
    out,
    row_offset, column_offset, slot_subgrid, row_taper, column_gain, held, coarse_r, coarse_i, fine_r, fine_i, steep_r, steep_i, encode, decode_r, decode_i,
    pair_out, pair_in, far_part, far_out, far_in, own_part, strip, strip_in,
    partial, mine, sums, slots_out, slots_in,
    small_sem, held_sem, pair_send, pair_recv, far_send, far_recv, strip_send, strip_recv, slot_send, slot_recv,
):
    col = lax.axis_index("col")
    fac = lax.axis_index("fac")
    col_hi, core = col // 2, col % 2
    fac_hi, fac_lo = fac // 2, fac % 2
    highs, zs = cols // 2, facs // 2
    rows, width = facets.shape[1], facets.shape[2]

    pair_id = (col_hi * 2 + 1 - core, fac)
    far_ids = [((col_hi + d) % highs * 2 + core, fac) for d in range(1, highs)]
    strip_id = (col, fac_hi * 2 + 1 - fac_lo)
    slot_ids = [(col, (fac_hi + d) % zs * 2 + fac_lo) for d in range(1, zs)]
    peers = [pair_id, *far_ids, strip_id, *slot_ids]
    own_columns = pl.ds(pl.multiple_of(fac * width, width), width)
    small = [
        pltpu.make_async_copy(source, target, small_sem.at[n])
        for n, (source, target) in enumerate((
            (row_offset_in, row_offset), (column_offset_in, column_offset), (slot_subgrid_in, slot_subgrid),
            (row_taper_in, row_taper),
            (column_taper_in.at[:, own_columns], column_gain)))]
    loads = [pltpu.make_async_copy(facets.at[p], held.at[p], held_sem.at[p]) for p in range(2)]
    for load in (*small, *loads):
        load.start()
    barrier = pltpu.get_barrier_semaphore()
    for peer in peers:
        pl.semaphore_signal(barrier, inc=1, device_id=peer, device_id_type=MESH)

    steps = STRIP // FINE
    position = col * rows + iota((1, rows), 1)
    fine_r[...], fine_i[...] = unit_phase(iota((FINE, rows), 0) * position)
    for load in small:
        load.wait()
    gain = row_taper[...] * (1.0 / math.sqrt(FACET))

    def coarse(own, group):
        first = (row_offset[group] + FINE * iota((steps, rows), 0)) & (FACET - 1)
        real, imag = unit_phase(first * position)
        coarse_r[own] = real * gain
        coarse_i[own] = imag * gain

    def encode_half(index, own, half):
        def row(i, carry):
            source = pl.ds(half * (steps // HALVES) + i, 1)
            ar, ai = coarse_r[own, source, :], coarse_i[own, source, :]
            br, bi = fine_r[...], fine_i[...]
            at = pl.multiple_of(i * FINE, FINE) + half * 2 * HALF
            encode[index, pl.ds(at, FINE), :] = (ar * br - ai * bi).astype(jnp.bfloat16)
            encode[index, pl.ds(at + HALF, FINE), :] = (ar * bi + ai * br).astype(jnp.bfloat16)
            return carry

        lax.fori_loop(0, steps // HALVES, row, 0)

    def product(target, index, halves):
        table = encode[index, halves[0] * 2 * HALF:(halves[-1] + 1) * 2 * HALF]
        by_real, by_imag = [jnp.dot(table, held[p], preferred_element_type=jnp.float32) for p in range(2)]
        for n, half in enumerate(halves):
            at = n * 2 * HALF
            real = by_real[at:at + HALF] - by_imag[at + HALF:at + 2 * HALF]
            imag = by_imag[at:at + HALF] + by_real[at + HALF:at + 2 * HALF]
            for j in chunks_of(half):
                begin, size = span(j).start, SIZES[j]
                first = begin // 2 - half * HALF
                target[begin:begin + size] = real[first:first + size].astype(target.dtype)
                target[begin + size:begin + 2 * size] = imag[first:first + size].astype(target.dtype)

    def sends(source, target, send, recv, peer):
        return pltpu.make_async_remote_copy(
            src_ref=source, dst_ref=target, send_sem=send, recv_sem=recv, device_id=peer, device_id_type=MESH)

    def pair_copy(d, half):
        at = pl.ds(half * 2 * HALF, 2 * HALF)
        return sends(pair_out.at[d, at], pair_in.at[d, at], pair_send.at[0], pair_recv.at[d, half], pair_id)

    def far_copy(d, j):
        return sends(
            far_out.at[d - 1, span(j)], far_in.at[d - 1, span(j)], far_send.at[0], far_recv.at[d - 1, j], far_ids[d - 1])

    def strip_copy(j):
        return sends(strip.at[span(j)], strip_in.at[span(j)], strip_send.at[0], strip_recv.at[j], strip_id)

    def slot_copy(d, j):
        return sends(
            slots_out.at[d - 1, span(j)], slots_in.at[d - 1, span(j)], slot_send.at[0], slot_recv.at[j // (CHUNKS - 1)], slot_ids[d - 1])

    def slots_wait(last):
        edge = span(CHUNKS - 1).start
        at = slice(edge, 2 * STRIP) if last else slice(0, edge)
        sends(slots_out.at[:, at], slots_in.at[:, at], slot_send.at[0], slot_recv.at[last], strip_id).wait_recv()

    whole = range(HALVES)

    def group_of(d, own):
        return (col_hi + d) % highs * 2 + (core if own else 1 - core)

    def relay(d, half):
        pair_copy(d, half).wait_recv()
        for j in chunks_of(half):
            far_out[d - 1, span(j)] = (
                far_part[d - 1, span(j)] + pair_in[d, span(j)].astype(jnp.float32)).astype(jnp.bfloat16)
            far_copy(d, j).start()

    def send_pair(d, halves):
        for half in halves:
            pair_copy(d, half).start()

    def near(d, half):
        product(pair_out.at[d], 2 * d, [half])
        send_pair(d, [half])

    def far(d, half):
        product(far_part.at[d - 1], 2 * d + 1, [half])

    def table(d, own):
        coarse(own, group_of(d, own))
        encode_half(2 * d + own, own, 0)

    def enter(d):
        if d == 1:
            pl.semaphore_wait(barrier, len(peers))

    def ready(d):
        if d == 1:
            for load in loads:
                load.wait()

    @pl.when(core == 0)
    def _():
        for d in range(1, highs):
            table(d, 1)
            ready(d)
            far(d, 0)
            enter(d)
            table(d, 0)
            relay(d, 0)
            near(d, 0)
            for own in range(2):
                encode_half(2 * d + own, own, 1)
            far(d, 1)
            near(d, 1)
            relay(d, 1)

    @pl.when(core == 1)
    def _():
        for d in range(1, highs):
            table(d, 0)
            ready(d)
            product(pair_out.at[d], 2 * d, [0])
            enter(d)
            send_pair(d, [0])
            table(d, 1)
            far(d, 0)
            for own in range(2):
                encode_half(2 * d + own, own, 1)
            near(d, 1)
            far(d, 1)

    def relays(half):
        @pl.when(core == 1)
        def _():
            for d in range(1, highs):
                relay(d, half)

    table(0, 0)
    encode_half(0, 0, 1)
    relays(0)
    product(pair_out.at[0], 0, whole)
    send_pair(0, whole)
    table(0, 1)
    encode_half(1, 1, 1)
    relays(1)
    product(own_part, 1, whole)

    def decoded(block):
        size = block.shape[0] // 2
        by_real = jnp.dot(block, decode_r[...], preferred_element_type=jnp.float32)
        by_imag = jnp.dot(block, decode_i[...], preferred_element_type=jnp.float32)
        return by_real[:size] - by_imag[size:], by_imag[:size] + by_real[size:]

    def arrive(j):
        if j in [chunks_of(half)[0] for half in whole]:
            pair_copy(0, span(j).start // (2 * HALF)).wait_recv()
        total = own_part[span(j)] + pair_in[0, span(j)].astype(jnp.float32)
        for d in range(1, highs):
            far_copy(d, j).wait_recv()
            total = total + far_in[d - 1, span(j)].astype(jnp.float32)
        strip[span(j)] = (total * column_gain[...]).astype(jnp.bfloat16)
        strip_copy(j).start()

    def finish(j):
        strip_copy(j).wait_recv()
        real, imag = decoded(strip_in[span(j)])
        total = partial[span(j)] + jnp.concatenate(
            [real * turn[0] - imag * turn[1], imag * turn[0] + real * turn[1]], axis=0)
        mine[span(j)] = total[:, :STRIP]
        for d in range(1, zs):
            slots_out[d - 1, span(j)] = total[:, d * STRIP:(d + 1) * STRIP].astype(jnp.bfloat16)
            slot_copy(d, j).start()

    turn = []

    def decode_tables():
        lanes = zs * STRIP
        coarse_n = width // FINE
        starts = []
        for d in range(zs):
            start = column_offset[slot_subgrid[col, (fac_hi + d) % zs * 2 + fac_lo]]
            starts.append((start + iota((1, STRIP), 1)) & (FACET - 1))
        frequency = jnp.concatenate(starts, axis=1)
        fine_real, fine_imag = unit_phase(iota((FINE, lanes), 0) * frequency)
        fine_real, fine_imag = fine_real * (1.0 / math.sqrt(FACET)), fine_imag * (1.0 / math.sqrt(FACET))
        steep_r[...], steep_i[...] = unit_phase((fac * width + FINE * iota((coarse_n, lanes), 0)) * frequency)
        shift_real, shift_imag = unit_phase((1 - 2 * fac_lo) * width * frequency)

        def row(i, carry):
            ar, ai = steep_r[pl.ds(i, 1), :], steep_i[pl.ds(i, 1), :]
            at = pl.multiple_of(i * FINE, FINE)
            decode_r[pl.ds(at, FINE), :] = (ar * fine_real - ai * fine_imag).astype(jnp.bfloat16)
            decode_i[pl.ds(at, FINE), :] = (ar * fine_imag + ai * fine_real).astype(jnp.bfloat16)
            return carry

        lax.fori_loop(0, coarse_n, row, 0)
        turn.extend((shift_real, shift_imag))

    for stage, j in order():
        if stage == 0:
            arrive(j)
            if j == LEAD:
                decode_tables()
            for done in range(j + 1) if j == LEAD else [j] if j > LEAD else []:
                partial[span(done)] = jnp.concatenate(decoded(strip[span(done)]), axis=0)
        else:
            finish(j)

    sends(pair_out, pair_in, pair_send.at[0], pair_recv.at[0, 0], pair_id).wait_send()
    if highs > 1:
        sends(far_out, far_in, far_send.at[0], far_recv.at[0, 0], far_ids[0]).wait_send()
    sends(strip, strip_in, strip_send.at[0], strip_recv.at[0], strip_id).wait_send()
    for j, size in enumerate(SIZES):
        total = mine[span(j)]
        if j in (0, CHUNKS - 1):
            slots_wait(j // (CHUNKS - 1))
        for d in range(1, zs):
            total = total + slots_in[d - 1, span(j)].astype(jnp.float32)
        first = span(j).start // 2
        for p in range(2):
            sums[p, first:first + size] = total[p * size:(p + 1) * size]
    for p in range(2):
        out[p] = sums[p].T
    sends(slots_out, slots_in, slot_send.at[0], slot_recv.at[0], strip_id).wait_send()


def place_kernel(place, part, out, grid, sem):
    shift = lax.rem(place[0], 8)
    first = pl.multiple_of(place[0] - shift, 8)
    band = STRIP + 8
    copies = [pltpu.make_async_copy(grid.at[n, pl.ds(0, SUBGRID)], out.at[n], sem.at[n]) for n in range(2)]
    for n in range(2):
        grid[n] = jnp.zeros(grid.shape[1:], jnp.float32)
        grid[n, pl.ds(first, band)] = pltpu.roll(
            jnp.concatenate([part[n], jnp.zeros((8, STRIP), jnp.float32)], axis=0), shift, 0)
        grid[n, :band] += grid[n, SUBGRID:]
        copies[n].start()
    for copy in copies:
        copy.wait()


def solution(mesh):
    cols, facs = mesh.shape["col"], mesh.shape["fac"]
    highs, zs = cols // 2, facs // 2

    def on_device(facets, row_taper, column_taper, column_place, row_offset, column_offset, slot_subgrid):
        rows, width = facets.shape[1], facets.shape[2]
        bf16, f32 = jnp.bfloat16, jnp.float32
        lanes = zs * STRIP
        part = (2 * STRIP, width)
        slot = (2 * STRIP, STRIP)
        far = max(highs - 1, 1)
        sem = pltpu.SemaphoreType.DMA
        grid = pl.pallas_call(
            functools.partial(kernel, cols, facs),
            out_shape=jax.ShapeDtypeStruct((2, STRIP, STRIP), f32),
            in_specs=[pl.BlockSpec(memory_space=pltpu.HBM)] * 6,
            out_specs=pl.BlockSpec(memory_space=pltpu.VMEM),
            scratch_shapes=[
                pltpu.SMEM(row_offset.shape, jnp.int32), pltpu.SMEM(column_offset.shape, jnp.int32),
                pltpu.SMEM(slot_subgrid.shape, jnp.int32),
                pltpu.VMEM((1, rows), f32), pltpu.VMEM((1, width), f32),
                pltpu.VMEM((2, rows, width), bf16),
                pltpu.VMEM((2, STRIP // FINE, rows), f32), pltpu.VMEM((2, STRIP // FINE, rows), f32),
                pltpu.VMEM((FINE, rows), f32), pltpu.VMEM((FINE, rows), f32),
                pltpu.VMEM((width // FINE, lanes), f32), pltpu.VMEM((width // FINE, lanes), f32),
                pltpu.VMEM((cols, 2 * STRIP, rows), bf16),
                pltpu.VMEM((width, lanes), bf16), pltpu.VMEM((width, lanes), bf16),
                pltpu.VMEM((highs, *part), bf16), pltpu.VMEM((highs, *part), bf16),
                pltpu.VMEM((far, *part), f32),
                pltpu.VMEM((far, *part), bf16), pltpu.VMEM((far, *part), bf16),
                pltpu.VMEM(part, f32),
                pltpu.VMEM(part, bf16), pltpu.VMEM(part, bf16),
                pltpu.VMEM((2 * STRIP, lanes), f32),
                pltpu.VMEM(slot, f32), pltpu.VMEM((2, STRIP, STRIP), f32),
                pltpu.VMEM((zs - 1, *slot), bf16), pltpu.VMEM((zs - 1, *slot), bf16),
                sem((5,)), sem((2,)),
                sem((1,)), sem((highs, HALVES)),
                sem((1,)), sem((far, CHUNKS)),
                sem((1,)), sem((CHUNKS,)),
                sem((1,)), sem((2,)),
            ],
            compiler_params=pltpu.CompilerParams(
                collective_id=0, has_side_effects=True, vmem_limit_bytes=32 * 1024 * 1024),
        )(*[pltpu.with_memory_space_constraint(value, pltpu.HBM) for value in (
            row_offset, column_offset, slot_subgrid, row_taper.reshape(1, -1), column_taper.reshape(1, -1), facets)])
        grid = pl.pallas_call(
            place_kernel,
            out_shape=jax.ShapeDtypeStruct((2, SUBGRID, STRIP), f32),
            in_specs=[pl.BlockSpec(memory_space=pltpu.SMEM), pl.BlockSpec(memory_space=pltpu.VMEM)],
            out_specs=pl.BlockSpec(memory_space=pltpu.HBM),
            scratch_shapes=[pltpu.VMEM((2, SUBGRID + STRIP + 8, STRIP), f32), sem((2,))],
            compiler_params=pltpu.CompilerParams(vmem_limit_bytes=8 * 1024 * 1024),
        )(column_place, grid)
        return grid.reshape(1, 1, 2, SUBGRID, STRIP)

    in_specs = (P(None, "col", "fac"), P("col"), P(), P(), P(), P(), P())
    out_specs = P("col", "fac", None, None, None)
    return jax.shard_map(on_device, mesh=mesh, in_specs=in_specs, out_specs=out_specs, check_vma=False)
```

```python
import functools
import math

import jax
import jax.numpy as jnp
from jax import lax
from jax.experimental import pallas as pl
from jax.experimental.pallas import tpu as pltpu
from jax.sharding import PartitionSpec as P

FACET = 4096
STRIP = 128
SUBGRID = 512
FINE = 16
SIZES = (16, 16, 16, 16, 16, 16, 16, 16)
CHUNKS = len(SIZES)
HOP_ROWS = 68
LEAD = 2
HALVES = 2
HALF = STRIP // HALVES
MESH = pl.DeviceIdType.MESH


def unit_phase(phases):
    quarter = FACET // 4
    shifted = phases + quarter // 2
    angle = ((shifted & (quarter - 1)) - quarter // 2).astype(jnp.float32) * (2.0 * math.pi / FACET)
    turn = lax.shift_right_logical(shifted & (FACET - 1), quarter.bit_length() - 1)
    sq = angle * angle
    cosine = 1.0 + sq * (-1 / 2 + sq * (1 / 24 + sq * (-1 / 720 + sq * (1 / 40320))))
    sine = angle * (1.0 + sq * (-1 / 6 + sq * (1 / 120 + sq * (-1 / 5040 + sq * (1 / 362880)))))
    odd = (turn & 1) == 1
    first = jnp.where(odd, sine, cosine)
    second = jnp.where(odd, cosine, sine)
    real = jnp.where(((turn + 1) & 2) == 2, -first, first)
    imag = jnp.where((turn & 2) == 2, second, -second)
    return real, imag


def span(j):
    start = 2 * sum(SIZES[:j])
    return slice(start, start + 2 * SIZES[j])


def order():
    far_done, free, events = 0, 0, []
    for j, size in enumerate(SIZES):
        far_done += size
        free = max(free, far_done) + size
        events += [(far_done, 0, j), (free + HOP_ROWS, 1, j)]
    return [event[1:] for event in sorted(events)]


def chunks_of(half):
    return [j for j in range(CHUNKS) if sum(SIZES[:j]) // HALF == half]


def iota(shape, dim):
    return lax.broadcasted_iota(jnp.int32, shape, dim)


def kernel(
    cols, facs,
    row_offset_in, column_offset_in, slot_subgrid_in, row_taper_in, column_taper_in, facets,
    out,
    row_offset, column_offset, slot_subgrid, row_taper, column_gain, held, coarse_r, coarse_i, fine_r, fine_i, steep_r, steep_i, encode, decode_r, decode_i,
    pair_out, pair_in, far_part, far_out, far_in, own_part, strip, strip_in,
    partial, mine, sums, slots_out, slots_in,
    small_sem, held_sem, pair_send, pair_recv, far_send, far_recv, strip_send, strip_recv, slot_send, slot_recv,
):
    col = lax.axis_index("col")
    fac = lax.axis_index("fac")
    col_hi, core = col // 2, col % 2
    fac_hi, fac_lo = fac // 2, fac % 2
    highs, zs = cols // 2, facs // 2
    rows, width = facets.shape[1], facets.shape[2]

    pair_id = (col_hi * 2 + 1 - core, fac)
    far_ids = [((col_hi + d) % highs * 2 + core, fac) for d in range(1, highs)]
    strip_id = (col, fac_hi * 2 + 1 - fac_lo)
    slot_ids = [(col, (fac_hi + d) % zs * 2 + fac_lo) for d in range(1, zs)]
    peers = [pair_id, *far_ids, strip_id, *slot_ids]
    own_columns = pl.ds(pl.multiple_of(fac * width, width), width)
    small = [
        pltpu.make_async_copy(source, target, small_sem.at[n])
        for n, (source, target) in enumerate((
            (row_offset_in, row_offset), (column_offset_in, column_offset), (slot_subgrid_in, slot_subgrid),
            (row_taper_in, row_taper),
            (column_taper_in.at[:, own_columns], column_gain)))]
    loads = [pltpu.make_async_copy(facets.at[p, pl.ds(q * rows // 4, rows // 4)], held.at[p, pl.ds(q * rows // 4, rows // 4)], held_sem.at[4 * p + q]) for p in range(2) for q in range(4)]
    for load in (*small, *loads):
        load.start()
    barrier = pltpu.get_barrier_semaphore()
    for peer in peers:
        pl.semaphore_signal(barrier, inc=1, device_id=peer, device_id_type=MESH)

    steps = STRIP // FINE
    position = col * rows + iota((1, rows), 1)
    fine_r[...], fine_i[...] = unit_phase(iota((FINE, rows), 0) * position)
    for load in small:
        load.wait()
    gain = row_taper[...] * (1.0 / math.sqrt(FACET))

    def coarse(own, group):
        first = (row_offset[group] + FINE * iota((steps, rows), 0)) & (FACET - 1)
        real, imag = unit_phase(first * position)
        coarse_r[own] = real * gain
        coarse_i[own] = imag * gain

    def encode_half(index, own, half):
        def row(i, carry):
            source = pl.ds(half * (steps // HALVES) + i, 1)
            ar, ai = coarse_r[own, source, :], coarse_i[own, source, :]
            br, bi = fine_r[...], fine_i[...]
            at = pl.multiple_of(i * FINE, FINE) + half * 2 * HALF
            encode[index, pl.ds(at, FINE), :] = (ar * br - ai * bi).astype(jnp.bfloat16)
            encode[index, pl.ds(at + HALF, FINE), :] = (ar * bi + ai * br).astype(jnp.bfloat16)
            return carry

        lax.fori_loop(0, steps // HALVES, row, 0)

    def product(target, index, halves):
        table = encode[index, halves[0] * 2 * HALF:(halves[-1] + 1) * 2 * HALF]
        by_real, by_imag = [jnp.dot(table, held[p], preferred_element_type=jnp.float32) for p in range(2)]
        for n, half in enumerate(halves):
            at = n * 2 * HALF
            real = by_real[at:at + HALF] - by_imag[at + HALF:at + 2 * HALF]
            imag = by_imag[at:at + HALF] + by_real[at + HALF:at + 2 * HALF]
            for j in chunks_of(half):
                begin, size = span(j).start, SIZES[j]
                first = begin // 2 - half * HALF
                target[begin:begin + size] = real[first:first + size].astype(target.dtype)
                target[begin + size:begin + 2 * size] = imag[first:first + size].astype(target.dtype)

    def sends(source, target, send, recv, peer):
        return pltpu.make_async_remote_copy(
            src_ref=source, dst_ref=target, send_sem=send, recv_sem=recv, device_id=peer, device_id_type=MESH)

    def pair_copy(d, half):
        at = pl.ds(half * 2 * HALF, 2 * HALF)
        return sends(pair_out.at[d, at], pair_in.at[d, at], pair_send.at[0], pair_recv.at[d, half], pair_id)

    def far_copy(d, j):
        return sends(
            far_out.at[d - 1, span(j)], far_in.at[d - 1, span(j)], far_send.at[0], far_recv.at[d - 1, j], far_ids[d - 1])

    def strip_copy(j):
        return sends(strip.at[span(j)], strip_in.at[span(j)], strip_send.at[0], strip_recv.at[j], strip_id)

    def slot_copy(d, j):
        return sends(
            slots_out.at[d - 1, span(j)], slots_in.at[d - 1, span(j)], slot_send.at[0], slot_recv.at[j // (CHUNKS - 1)], slot_ids[d - 1])

    def slots_wait(last):
        edge = span(CHUNKS - 1).start
        at = slice(edge, 2 * STRIP) if last else slice(0, edge)
        sends(slots_out.at[:, at], slots_in.at[:, at], slot_send.at[0], slot_recv.at[last], strip_id).wait_recv()

    whole = range(HALVES)

    def group_of(d, own):
        return (col_hi + d) % highs * 2 + (core if own else 1 - core)

    def relay(d, half):
        pair_copy(d, half).wait_recv()
        for j in chunks_of(half):
            far_out[d - 1, span(j)] = (
                far_part[d - 1, span(j)] + pair_in[d, span(j)].astype(jnp.float32)).astype(jnp.bfloat16)
            far_copy(d, j).start()

    def send_pair(d, halves):
        for half in halves:
            pair_copy(d, half).start()

    def near(d, half):
        product(pair_out.at[d], 2 * d, [half])
        send_pair(d, [half])

    def far(d, half):
        product(far_part.at[d - 1], 2 * d + 1, [half])

    def table(d, own):
        coarse(own, group_of(d, own))
        encode_half(2 * d + own, own, 0)

    def enter(d):
        if d == 1:
            pl.semaphore_wait(barrier, len(peers))

    def ready(d):
        if d == 1:
            for load in loads:
                load.wait()

    @pl.when(core == 0)
    def _():
        for d in range(1, highs):
            table(d, 1)
            ready(d)
            far(d, 0)
            enter(d)
            table(d, 0)
            for own in range(2):
                encode_half(2 * d + own, own, 1)
            if d == highs - 1:
                table(0, 0)
                encode_half(0, 0, 1)
            relay(d, 0)
            near(d, 0)
            far(d, 1)
            near(d, 1)
            relay(d, 1)

    @pl.when(core == 1)
    def _():
        for d in range(1, highs):
            table(d, 0)
            ready(d)
            product(pair_out.at[d], 2 * d, [0])
            enter(d)
            send_pair(d, [0])
            table(d, 1)
            far(d, 0)
            for own in range(2):
                encode_half(2 * d + own, own, 1)
            near(d, 1)
            far(d, 1)
        table(0, 0)
        encode_half(0, 0, 1)

    def relays(half):
        @pl.when(core == 1)
        def _():
            for d in range(1, highs):
                relay(d, half)

    product(pair_out.at[0], 0, whole)
    send_pair(0, whole)
    relays(0)
    table(0, 1)
    encode_half(1, 1, 1)
    relays(1)
    product(own_part, 1, whole)

    def decoded(block):
        size = block.shape[0] // 2
        by_real = jnp.dot(block, decode_r[...], preferred_element_type=jnp.float32)
        by_imag = jnp.dot(block, decode_i[...], preferred_element_type=jnp.float32)
        return by_real[:size] - by_imag[size:], by_imag[:size] + by_real[size:]

    def arrive(j):
        if j in [chunks_of(half)[0] for half in whole]:
            pair_copy(0, span(j).start // (2 * HALF)).wait_recv()
        total = own_part[span(j)] + pair_in[0, span(j)].astype(jnp.float32)
        for d in range(1, highs):
            far_copy(d, j).wait_recv()
            total = total + far_in[d - 1, span(j)].astype(jnp.float32)
        strip[span(j)] = (total * column_gain[...]).astype(jnp.bfloat16)
        strip_copy(j).start()

    def finish(j):
        strip_copy(j).wait_recv()
        real, imag = decoded(strip_in[span(j)])
        total = partial[span(j)] + jnp.concatenate(
            [real * turn[0] - imag * turn[1], imag * turn[0] + real * turn[1]], axis=0)
        mine[span(j)] = total[:, :STRIP]
        for d in range(1, zs):
            slots_out[d - 1, span(j)] = total[:, d * STRIP:(d + 1) * STRIP].astype(jnp.bfloat16)
            slot_copy(d, j).start()

    turn = []

    def decode_tables():
        lanes = zs * STRIP
        coarse_n = width // FINE
        starts = []
        for d in range(zs):
            start = column_offset[slot_subgrid[col, (fac_hi + d) % zs * 2 + fac_lo]]
            starts.append((start + iota((1, STRIP), 1)) & (FACET - 1))
        frequency = jnp.concatenate(starts, axis=1)
        fine_real, fine_imag = unit_phase(iota((FINE, lanes), 0) * frequency)
        fine_real, fine_imag = fine_real * (1.0 / math.sqrt(FACET)), fine_imag * (1.0 / math.sqrt(FACET))
        steep_r[...], steep_i[...] = unit_phase((fac * width + FINE * iota((coarse_n, lanes), 0)) * frequency)
        shift_real, shift_imag = unit_phase((1 - 2 * fac_lo) * width * frequency)

        def row(i, carry):
            ar, ai = steep_r[pl.ds(i, 1), :], steep_i[pl.ds(i, 1), :]
            at = pl.multiple_of(i * FINE, FINE)
            decode_r[pl.ds(at, FINE), :] = (ar * fine_real - ai * fine_imag).astype(jnp.bfloat16)
            decode_i[pl.ds(at, FINE), :] = (ar * fine_imag + ai * fine_real).astype(jnp.bfloat16)
            return carry

        lax.fori_loop(0, coarse_n, row, 0)
        turn.extend((shift_real, shift_imag))

    for stage, j in order():
        if stage == 0:
            arrive(j)
            if j == LEAD:
                decode_tables()
            for done in range(j + 1) if j == LEAD else [j] if j > LEAD else []:
                partial[span(done)] = jnp.concatenate(decoded(strip[span(done)]), axis=0)
        else:
            finish(j)

    sends(pair_out, pair_in, pair_send.at[0], pair_recv.at[0, 0], pair_id).wait_send()
    if highs > 1:
        sends(far_out, far_in, far_send.at[0], far_recv.at[0, 0], far_ids[0]).wait_send()
    sends(strip, strip_in, strip_send.at[0], strip_recv.at[0], strip_id).wait_send()
    for j, size in enumerate(SIZES):
        total = mine[span(j)]
        if j in (0, CHUNKS - 1):
            slots_wait(j // (CHUNKS - 1))
        for d in range(1, zs):
            total = total + slots_in[d - 1, span(j)].astype(jnp.float32)
        first = span(j).start // 2
        for p in range(2):
            sums[p, first:first + size] = total[p * size:(p + 1) * size]
    for p in range(2):
        out[p] = sums[p].T
    sends(slots_out, slots_in, slot_send.at[0], slot_recv.at[0], strip_id).wait_send()


def place_kernel(place, part, out, grid, sem):
    shift = lax.rem(place[0], 8)
    first = pl.multiple_of(place[0] - shift, 8)
    band = STRIP + 8
    copies = [pltpu.make_async_copy(grid.at[n, pl.ds(0, SUBGRID)], out.at[n], sem.at[n]) for n in range(2)]
    for n in range(2):
        grid[n] = jnp.zeros(grid.shape[1:], jnp.float32)
        grid[n, pl.ds(first, band)] = pltpu.roll(
            jnp.concatenate([part[n], jnp.zeros((8, STRIP), jnp.float32)], axis=0), shift, 0)
        grid[n, :band] += grid[n, SUBGRID:]
        copies[n].start()
    for copy in copies:
        copy.wait()


def solution(mesh):
    cols, facs = mesh.shape["col"], mesh.shape["fac"]
    highs, zs = cols // 2, facs // 2

    def on_device(facets, row_taper, column_taper, column_place, row_offset, column_offset, slot_subgrid):
        rows, width = facets.shape[1], facets.shape[2]
        bf16, f32 = jnp.bfloat16, jnp.float32
        lanes = zs * STRIP
        part = (2 * STRIP, width)
        slot = (2 * STRIP, STRIP)
        far = max(highs - 1, 1)
        sem = pltpu.SemaphoreType.DMA
        grid = pl.pallas_call(
            functools.partial(kernel, cols, facs),
            out_shape=jax.ShapeDtypeStruct((2, STRIP, STRIP), f32),
            in_specs=[pl.BlockSpec(memory_space=pltpu.HBM)] * 6,
            out_specs=pl.BlockSpec(memory_space=pltpu.VMEM),
            scratch_shapes=[
                pltpu.SMEM(row_offset.shape, jnp.int32), pltpu.SMEM(column_offset.shape, jnp.int32),
                pltpu.SMEM(slot_subgrid.shape, jnp.int32),
                pltpu.VMEM((1, rows), f32), pltpu.VMEM((1, width), f32),
                pltpu.VMEM((2, rows, width), bf16),
                pltpu.VMEM((2, STRIP // FINE, rows), f32), pltpu.VMEM((2, STRIP // FINE, rows), f32),
                pltpu.VMEM((FINE, rows), f32), pltpu.VMEM((FINE, rows), f32),
                pltpu.VMEM((width // FINE, lanes), f32), pltpu.VMEM((width // FINE, lanes), f32),
                pltpu.VMEM((cols, 2 * STRIP, rows), bf16),
                pltpu.VMEM((width, lanes), bf16), pltpu.VMEM((width, lanes), bf16),
                pltpu.VMEM((highs, *part), bf16), pltpu.VMEM((highs, *part), bf16),
                pltpu.VMEM((far, *part), f32),
                pltpu.VMEM((far, *part), bf16), pltpu.VMEM((far, *part), bf16),
                pltpu.VMEM(part, f32),
                pltpu.VMEM(part, bf16), pltpu.VMEM(part, bf16),
                pltpu.VMEM((2 * STRIP, lanes), f32),
                pltpu.VMEM(slot, f32), pltpu.VMEM((2, STRIP, STRIP), f32),
                pltpu.VMEM((zs - 1, *slot), bf16), pltpu.VMEM((zs - 1, *slot), bf16),
                sem((5,)), sem((8,)),
                sem((1,)), sem((highs, HALVES)),
                sem((1,)), sem((far, CHUNKS)),
                sem((1,)), sem((CHUNKS,)),
                sem((1,)), sem((2,)),
            ],
            compiler_params=pltpu.CompilerParams(
                collective_id=0, has_side_effects=True, vmem_limit_bytes=32 * 1024 * 1024),
        )(*[pltpu.with_memory_space_constraint(value, pltpu.HBM) for value in (
            row_offset, column_offset, slot_subgrid, row_taper.reshape(1, -1), column_taper.reshape(1, -1), facets)])
        grid = pl.pallas_call(
            place_kernel,
            out_shape=jax.ShapeDtypeStruct((2, SUBGRID, STRIP), f32),
            in_specs=[pl.BlockSpec(memory_space=pltpu.SMEM), pl.BlockSpec(memory_space=pltpu.VMEM)],
            out_specs=pl.BlockSpec(memory_space=pltpu.HBM),
            scratch_shapes=[pltpu.VMEM((2, SUBGRID + STRIP + 8, STRIP), f32), sem((2,))],
            compiler_params=pltpu.CompilerParams(vmem_limit_bytes=8 * 1024 * 1024),
        )(column_place, grid)
        return grid.reshape(1, 1, 2, SUBGRID, STRIP)

    in_specs = (P(None, "col", "fac"), P("col"), P(), P(), P(), P(), P())
    out_specs = P("col", "fac", None, None, None)
    return jax.shard_map(on_device, mesh=mesh, in_specs=in_specs, out_specs=out_specs, check_vma=False)
```

```python
import functools
import math

import jax
import jax.numpy as jnp
from jax import lax
from jax.experimental import pallas as pl
from jax.experimental.pallas import tpu as pltpu
from jax.sharding import PartitionSpec as P

FACET = 4096
STRIP = 128
SUBGRID = 512
FINE = 16
SIZES = (16, 16, 16, 16, 16, 16, 16, 16)
CHUNKS = len(SIZES)
HOP_ROWS = 48
LEAD = 2
HALVES = 2
HALF = STRIP // HALVES
MESH = pl.DeviceIdType.MESH


def unit_phase(phases):
    quarter = FACET // 4
    shifted = phases + quarter // 2
    angle = ((shifted & (quarter - 1)) - quarter // 2).astype(jnp.float32) * (2.0 * math.pi / FACET)
    turn = lax.shift_right_logical(shifted & (FACET - 1), quarter.bit_length() - 1)
    sq = angle * angle
    cosine = 1.0 + sq * (-1 / 2 + sq * (1 / 24 + sq * (-1 / 720 + sq * (1 / 40320))))
    sine = angle * (1.0 + sq * (-1 / 6 + sq * (1 / 120 + sq * (-1 / 5040 + sq * (1 / 362880)))))
    odd = (turn & 1) == 1
    first = jnp.where(odd, sine, cosine)
    second = jnp.where(odd, cosine, sine)
    real = jnp.where(((turn + 1) & 2) == 2, -first, first)
    imag = jnp.where((turn & 2) == 2, second, -second)
    return real, imag


def span(j):
    start = 2 * sum(SIZES[:j])
    return slice(start, start + 2 * SIZES[j])


def order():
    far_done, free, events = 0, 0, []
    for j, size in enumerate(SIZES):
        far_done += size
        free = max(free, far_done) + size
        events += [(far_done, 0, j), (free + HOP_ROWS, 1, j)]
    return [event[1:] for event in sorted(events)]


def chunks_of(half):
    return [j for j in range(CHUNKS) if sum(SIZES[:j]) // HALF == half]


def iota(shape, dim):
    return lax.broadcasted_iota(jnp.int32, shape, dim)


def kernel(
    cols, facs,
    row_offset_in, column_offset_in, slot_subgrid_in, row_taper_in, column_taper_in, facets,
    out,
    row_offset, column_offset, slot_subgrid, row_taper, column_gain, held, coarse_r, coarse_i, fine_r, fine_i, steep_r, steep_i, encode, decode_r, decode_i,
    pair_out, pair_in, far_part, far_out, far_in, own_part, strip, strip_in,
    partial, mine, sums, slots_out, slots_in,
    small_sem, held_sem, pair_send, pair_recv, far_send, far_recv, strip_send, strip_recv, slot_send, slot_recv,
):
    col = lax.axis_index("col")
    fac = lax.axis_index("fac")
    col_hi, core = col // 2, col % 2
    fac_hi, fac_lo = fac // 2, fac % 2
    highs, zs = cols // 2, facs // 2
    rows, width = facets.shape[1], facets.shape[2]

    pair_id = (col_hi * 2 + 1 - core, fac)
    far_ids = [((col_hi + d) % highs * 2 + core, fac) for d in range(1, highs)]
    strip_id = (col, fac_hi * 2 + 1 - fac_lo)
    slot_ids = [(col, (fac_hi + d) % zs * 2 + fac_lo) for d in range(1, zs)]
    peers = [pair_id, *far_ids, strip_id, *slot_ids]
    own_columns = pl.ds(pl.multiple_of(fac * width, width), width)
    small = [
        pltpu.make_async_copy(source, target, small_sem.at[n])
        for n, (source, target) in enumerate((
            (row_offset_in, row_offset), (column_offset_in, column_offset), (slot_subgrid_in, slot_subgrid),
            (row_taper_in, row_taper),
            (column_taper_in.at[:, own_columns], column_gain)))]
    loads = [pltpu.make_async_copy(facets.at[p], held.at[p], held_sem.at[p]) for p in range(2)]
    for load in (*small, *loads):
        load.start()
    barrier = pltpu.get_barrier_semaphore()
    for peer in peers:
        pl.semaphore_signal(barrier, inc=1, device_id=peer, device_id_type=MESH)

    steps = STRIP // FINE
    position = col * rows + iota((1, rows), 1)
    fine_r[...], fine_i[...] = unit_phase(iota((FINE, rows), 0) * position)
    for load in small:
        load.wait()
    gain = row_taper[...] * (1.0 / math.sqrt(FACET))

    def coarse(own, group):
        first = (row_offset[group] + FINE * iota((steps, rows), 0)) & (FACET - 1)
        real, imag = unit_phase(first * position)
        coarse_r[own] = real * gain
        coarse_i[own] = imag * gain

    def encode_half(index, own, half):
        def row(i, carry):
            source = pl.ds(half * (steps // HALVES) + i, 1)
            ar, ai = coarse_r[own, source, :], coarse_i[own, source, :]
            br, bi = fine_r[...], fine_i[...]
            at = pl.multiple_of(i * FINE, FINE) + half * 2 * HALF
            encode[index, pl.ds(at, FINE), :] = (ar * br - ai * bi).astype(jnp.bfloat16)
            encode[index, pl.ds(at + HALF, FINE), :] = (ar * bi + ai * br).astype(jnp.bfloat16)
            return carry

        lax.fori_loop(0, steps // HALVES, row, 0)

    def product(target, index, halves):
        table = encode[index, halves[0] * 2 * HALF:(halves[-1] + 1) * 2 * HALF]
        by_real, by_imag = [jnp.dot(table, held[p], preferred_element_type=jnp.float32) for p in range(2)]
        for n, half in enumerate(halves):
            at = n * 2 * HALF
            real = by_real[at:at + HALF] - by_imag[at + HALF:at + 2 * HALF]
            imag = by_imag[at:at + HALF] + by_real[at + HALF:at + 2 * HALF]
            for j in chunks_of(half):
                begin, size = span(j).start, SIZES[j]
                first = begin // 2 - half * HALF
                target[begin:begin + size] = real[first:first + size].astype(target.dtype)
                target[begin + size:begin + 2 * size] = imag[first:first + size].astype(target.dtype)

    def sends(source, target, send, recv, peer):
        return pltpu.make_async_remote_copy(
            src_ref=source, dst_ref=target, send_sem=send, recv_sem=recv, device_id=peer, device_id_type=MESH)

    def pair_copy(d, half):
        at = pl.ds(half * 2 * HALF, 2 * HALF)
        return sends(pair_out.at[d, at], pair_in.at[d, at], pair_send.at[0], pair_recv.at[d, half], pair_id)

    def far_copy(d, j):
        return sends(
            far_out.at[d - 1, span(j)], far_in.at[d - 1, span(j)], far_send.at[0], far_recv.at[d - 1, j], far_ids[d - 1])

    def strip_copy(j):
        return sends(strip.at[span(j)], strip_in.at[span(j)], strip_send.at[0], strip_recv.at[j], strip_id)

    def slot_copy(d, j):
        return sends(
            slots_out.at[d - 1, span(j)], slots_in.at[d - 1, span(j)], slot_send.at[0], slot_recv.at[j // (CHUNKS - 1)], slot_ids[d - 1])

    def slots_wait(last):
        edge = span(CHUNKS - 1).start
        at = slice(edge, 2 * STRIP) if last else slice(0, edge)
        sends(slots_out.at[:, at], slots_in.at[:, at], slot_send.at[0], slot_recv.at[last], strip_id).wait_recv()

    whole = range(HALVES)

    def group_of(d, own):
        return (col_hi + d) % highs * 2 + (core if own else 1 - core)

    def relay(d, half):
        pair_copy(d, half).wait_recv()
        for j in chunks_of(half):
            far_out[d - 1, span(j)] = (
                far_part[d - 1, span(j)] + pair_in[d, span(j)].astype(jnp.float32)).astype(jnp.bfloat16)
            far_copy(d, j).start()

    def send_pair(d, halves):
        for half in halves:
            pair_copy(d, half).start()

    def near(d, half):
        product(pair_out.at[d], 2 * d, [half])
        send_pair(d, [half])

    def far(d, half):
        product(far_part.at[d - 1], 2 * d + 1, [half])

    def table(d, own):
        coarse(own, group_of(d, own))
        encode_half(2 * d + own, own, 0)

    def enter(d):
        if d == 1:
            pl.semaphore_wait(barrier, len(peers))

    def ready(d):
        if d == 1:
            for load in loads:
                load.wait()

    @pl.when(core == 0)
    def _():
        for d in range(1, highs):
            table(d, 1)
            ready(d)
            far(d, 0)
            enter(d)
            table(d, 0)
            for own in range(2):
                encode_half(2 * d + own, own, 1)
            if d == highs - 1:
                table(0, 0)
                encode_half(0, 0, 1)
            relay(d, 0)
            near(d, 0)
            far(d, 1)
            near(d, 1)
            relay(d, 1)

    @pl.when(core == 1)
    def _():
        for d in range(1, highs):
            table(d, 0)
            ready(d)
            product(pair_out.at[d], 2 * d, [0])
            enter(d)
            send_pair(d, [0])
            table(d, 1)
            far(d, 0)
            for own in range(2):
                encode_half(2 * d + own, own, 1)
            near(d, 1)
            far(d, 1)
        table(0, 0)
        encode_half(0, 0, 1)

    def relays(half):
        @pl.when(core == 1)
        def _():
            for d in range(1, highs):
                relay(d, half)

    product(pair_out.at[0], 0, whole)
    send_pair(0, whole)
    relays(0)
    table(0, 1)
    encode_half(1, 1, 1)
    relays(1)
    product(own_part, 1, whole)

    def decoded(block):
        size = block.shape[0] // 2
        by_real = jnp.dot(block, decode_r[...], preferred_element_type=jnp.float32)
        by_imag = jnp.dot(block, decode_i[...], preferred_element_type=jnp.float32)
        return by_real[:size] - by_imag[size:], by_imag[:size] + by_real[size:]

    def arrive(j):
        if j in [chunks_of(half)[0] for half in whole]:
            pair_copy(0, span(j).start // (2 * HALF)).wait_recv()
        total = own_part[span(j)] + pair_in[0, span(j)].astype(jnp.float32)
        for d in range(1, highs):
            far_copy(d, j).wait_recv()
            total = total + far_in[d - 1, span(j)].astype(jnp.float32)
        strip[span(j)] = (total * column_gain[...]).astype(jnp.bfloat16)
        strip_copy(j).start()

    def finish(j):
        strip_copy(j).wait_recv()
        real, imag = decoded(strip_in[span(j)])
        total = partial[span(j)] + jnp.concatenate(
            [real * turn[0] - imag * turn[1], imag * turn[0] + real * turn[1]], axis=0)
        mine[span(j)] = total[:, :STRIP]
        for d in range(1, zs):
            slots_out[d - 1, span(j)] = total[:, d * STRIP:(d + 1) * STRIP].astype(jnp.bfloat16)
            slot_copy(d, j).start()

    turn = []

    def decode_tables():
        lanes = zs * STRIP
        coarse_n = width // FINE
        starts = []
        for d in range(zs):
            start = column_offset[slot_subgrid[col, (fac_hi + d) % zs * 2 + fac_lo]]
            starts.append((start + iota((1, STRIP), 1)) & (FACET - 1))
        frequency = jnp.concatenate(starts, axis=1)
        fine_real, fine_imag = unit_phase(iota((FINE, lanes), 0) * frequency)
        fine_real, fine_imag = fine_real * (1.0 / math.sqrt(FACET)), fine_imag * (1.0 / math.sqrt(FACET))
        steep_r[...], steep_i[...] = unit_phase((fac * width + FINE * iota((coarse_n, lanes), 0)) * frequency)
        shift_real, shift_imag = unit_phase((1 - 2 * fac_lo) * width * frequency)

        def row(i, carry):
            ar, ai = steep_r[pl.ds(i, 1), :], steep_i[pl.ds(i, 1), :]
            at = pl.multiple_of(i * FINE, FINE)
            decode_r[pl.ds(at, FINE), :] = (ar * fine_real - ai * fine_imag).astype(jnp.bfloat16)
            decode_i[pl.ds(at, FINE), :] = (ar * fine_imag + ai * fine_real).astype(jnp.bfloat16)
            return carry

        lax.fori_loop(0, coarse_n, row, 0)
        turn.extend((shift_real, shift_imag))

    for stage, j in order():
        if stage == 0:
            arrive(j)
            if j == LEAD:
                decode_tables()
            for done in range(j + 1) if j == LEAD else [j] if j > LEAD else []:
                partial[span(done)] = jnp.concatenate(decoded(strip[span(done)]), axis=0)
        else:
            finish(j)

    sends(pair_out, pair_in, pair_send.at[0], pair_recv.at[0, 0], pair_id).wait_send()
    if highs > 1:
        sends(far_out, far_in, far_send.at[0], far_recv.at[0, 0], far_ids[0]).wait_send()
    sends(strip, strip_in, strip_send.at[0], strip_recv.at[0], strip_id).wait_send()
    for j, size in enumerate(SIZES):
        total = mine[span(j)]
        if j in (0, CHUNKS - 1):
            slots_wait(j // (CHUNKS - 1))
        for d in range(1, zs):
            total = total + slots_in[d - 1, span(j)].astype(jnp.float32)
        first = span(j).start // 2
        for p in range(2):
            sums[p, first:first + size] = total[p * size:(p + 1) * size]
    for p in range(2):
        out[p] = sums[p].T
    sends(slots_out, slots_in, slot_send.at[0], slot_recv.at[0], strip_id).wait_send()


def place_kernel(place, part, out, grid, sem):
    shift = lax.rem(place[0], 8)
    first = pl.multiple_of(place[0] - shift, 8)
    band = STRIP + 8
    copies = [pltpu.make_async_copy(grid.at[n, pl.ds(0, SUBGRID)], out.at[n], sem.at[n]) for n in range(2)]
    for n in range(2):
        grid[n] = jnp.zeros(grid.shape[1:], jnp.float32)
        grid[n, pl.ds(first, band)] = pltpu.roll(
            jnp.concatenate([part[n], jnp.zeros((8, STRIP), jnp.float32)], axis=0), shift, 0)
        grid[n, :band] += grid[n, SUBGRID:]
        copies[n].start()
    for copy in copies:
        copy.wait()


def solution(mesh):
    cols, facs = mesh.shape["col"], mesh.shape["fac"]
    highs, zs = cols // 2, facs // 2

    def on_device(facets, row_taper, column_taper, column_place, row_offset, column_offset, slot_subgrid):
        rows, width = facets.shape[1], facets.shape[2]
        bf16, f32 = jnp.bfloat16, jnp.float32
        lanes = zs * STRIP
        part = (2 * STRIP, width)
        slot = (2 * STRIP, STRIP)
        far = max(highs - 1, 1)
        sem = pltpu.SemaphoreType.DMA
        grid = pl.pallas_call(
            functools.partial(kernel, cols, facs),
            out_shape=jax.ShapeDtypeStruct((2, STRIP, STRIP), f32),
            in_specs=[pl.BlockSpec(memory_space=pltpu.HBM)] * 6,
            out_specs=pl.BlockSpec(memory_space=pltpu.VMEM),
            scratch_shapes=[
                pltpu.SMEM(row_offset.shape, jnp.int32), pltpu.SMEM(column_offset.shape, jnp.int32),
                pltpu.SMEM(slot_subgrid.shape, jnp.int32),
                pltpu.VMEM((1, rows), f32), pltpu.VMEM((1, width), f32),
                pltpu.VMEM((2, rows, width), bf16),
                pltpu.VMEM((2, STRIP // FINE, rows), f32), pltpu.VMEM((2, STRIP // FINE, rows), f32),
                pltpu.VMEM((FINE, rows), f32), pltpu.VMEM((FINE, rows), f32),
                pltpu.VMEM((width // FINE, lanes), f32), pltpu.VMEM((width // FINE, lanes), f32),
                pltpu.VMEM((cols, 2 * STRIP, rows), bf16),
                pltpu.VMEM((width, lanes), bf16), pltpu.VMEM((width, lanes), bf16),
                pltpu.VMEM((highs, *part), bf16), pltpu.VMEM((highs, *part), bf16),
                pltpu.VMEM((far, *part), f32),
                pltpu.VMEM((far, *part), bf16), pltpu.VMEM((far, *part), bf16),
                pltpu.VMEM(part, f32),
                pltpu.VMEM(part, bf16), pltpu.VMEM(part, bf16),
                pltpu.VMEM((2 * STRIP, lanes), f32),
                pltpu.VMEM(slot, f32), pltpu.VMEM((2, STRIP, STRIP), f32),
                pltpu.VMEM((zs - 1, *slot), bf16), pltpu.VMEM((zs - 1, *slot), bf16),
                sem((5,)), sem((2,)),
                sem((1,)), sem((highs, HALVES)),
                sem((1,)), sem((far, CHUNKS)),
                sem((1,)), sem((CHUNKS,)),
                sem((1,)), sem((2,)),
            ],
            compiler_params=pltpu.CompilerParams(
                collective_id=0, has_side_effects=True, vmem_limit_bytes=32 * 1024 * 1024),
        )(*[pltpu.with_memory_space_constraint(value, pltpu.HBM) for value in (
            row_offset, column_offset, slot_subgrid, row_taper.reshape(1, -1), column_taper.reshape(1, -1), facets)])
        grid = pl.pallas_call(
            place_kernel,
            out_shape=jax.ShapeDtypeStruct((2, SUBGRID, STRIP), f32),
            in_specs=[pl.BlockSpec(memory_space=pltpu.SMEM), pl.BlockSpec(memory_space=pltpu.VMEM)],
            out_specs=pl.BlockSpec(memory_space=pltpu.HBM),
            scratch_shapes=[pltpu.VMEM((2, SUBGRID + STRIP + 8, STRIP), f32), sem((2,))],
            compiler_params=pltpu.CompilerParams(vmem_limit_bytes=8 * 1024 * 1024),
        )(column_place, grid)
        return grid.reshape(1, 1, 2, SUBGRID, STRIP)

    in_specs = (P(None, "col", "fac"), P("col"), P(), P(), P(), P(), P())
    out_specs = P("col", "fac", None, None, None)
    return jax.shard_map(on_device, mesh=mesh, in_specs=in_specs, out_specs=out_specs, check_vma=False)
```
